32 devices in a mesh: gx: 4 (over y, x), gy: 8 (over z, core).
Axes of the slice: x: 2, y: 2, z: 4, core: 2. Of those that a mesh axis runs over, the one named last changes fastest.
Arguments:
- fields: float32 [6, 16, 128, 512], P(None, None, 'gy', 'gx'), may hold values from -4 to 4
- velocity: float32 [2, 16, 128, 512], P(None, None, 'gy', 'gx'), may hold values from -1 to 1
- coupling: float32 [6], replicated, may hold values from 0.5 to 4
- positions: float32 [3, 4, 8, 1024], P(None, 'gx', 'gy'), may hold values from 0 to 512, as said below
- log_radius: float32 [4, 8, 1024], P('gx', 'gy'), may hold values from -0.35 to 0.35
- growth: float32 [4, 8, 1024], P('gx', 'gy'), may hold values from -0.5 to 0.5
- rest_gap: float32 [4, 8, 1024], P('gx', 'gy'), may hold values from -0.15 to 0.15
- gas_pressure: float32 [4, 8, 1024], P('gx', 'gy'), may hold values from 0.7 to 1.4
- move_codes: int32 [4, 8, 1024], P('gx', 'gy'), may hold values from 0 to 9, as said below
- targets: int32 [4, 8, 1024], P('gx', 'gy'), may hold values from 0 to 1023, as said below
Outputs:
- new_fields: float32 [6, 16, 128, 512], P(None, None, 'gy', 'gx')
- new_bubbles: float32 [2, 4, 8, 1024], P(None, 'gx', 'gy')
The draws below stay inside these ranges and needn't reach their ends.
Inputs may be any that keep to these rules, and one draw needn't show every extreme that they name: `move_codes`: code 3 (a + 1) + (b + 1) sends the bubble to the tile a rows along gx and b columns along gy (a, b in -1, 0, 1); 4 keeps it; 9 marks an empty slot. No bubble leaves the plane. At most 128 bubbles of one tile carry the same code other than 4 and 9, and in every draw each tile sends exactly 128 to one neighbour. Among all bubbles bound for one tile the targets are distinct; for empty slots (code 9) the target is 0 and means nothing. `positions`: A bubble's x lies in [a * 128, (a + 1) * 128] and its y in [b * 16, (b + 1) * 16] for its destination tile (a, b); z lies in [0, 16).
All inputs are finite; a program needn't handle non-finite values.
Results may differ from the reference program's by a relative error of at most 0.0003.
Values sent between devices are 32-bit elements; how exact they have to be, the bound alone decides.
A program may use at most 64 MiB of HBM per device.

```python
import math
import jax
import jax.numpy as jnp
from jax import lax

NF = 6
CZ = 16
CX = 128
CY = 16
SLOTS = 1024
NX = 512
NY = 128
N_GX = 4
N_GY = 8


def bubble_plan(key):
    key = jax.random.fold_in(key, 4242)
    subkeys = jax.random.split(key, 6)
    capacity = SLOTS // 8
    grid_x = jnp.arange(N_GX, dtype=jnp.int32)[:, None, None]
    grid_y = jnp.arange(N_GY, dtype=jnp.int32)[None, :, None]
    heading_all = jnp.arange(9, dtype=jnp.int32)[None, None, :]
    step_x = heading_all // 3 - 1
    step_y = heading_all % 3 - 1
    allowed = (grid_x + step_x >= 0) & (grid_x + step_x < N_GX) & (grid_y + step_y >= 0) & (grid_y + step_y < N_GY) & (heading_all != 4)
    counts = jax.random.randint(subkeys[0], (N_GX, N_GY, 9), 0, capacity + 1) * allowed.astype(jnp.int32)
    scores = jax.random.randint(subkeys[1], (N_GX, N_GY, 9), 0, 1 << 20) * 16 + heading_all
    scores = jnp.where(allowed, scores, -1)
    chosen = jnp.argmax(scores, axis=-1).astype(jnp.int32)
    counts = jnp.where(heading_all == chosen[:, :, None], capacity, counts)
    padded = jnp.pad(counts, ((1, 1), (1, 1), (0, 0)))
    incoming = jnp.stack([padded[1 - (heading // 3 - 1):1 - (heading // 3 - 1) + N_GX, 1 - (heading % 3 - 1):1 - (heading % 3 - 1) + N_GY, heading] for heading in range(9)], axis=-1)
    leaving = jnp.sum(counts, axis=-1)
    arriving = jnp.sum(incoming, axis=-1)
    free_room = SLOTS - jnp.maximum(leaving, arriving)
    staying = jax.random.randint(subkeys[2], (N_GX, N_GY), 0, free_room + 1)
    counts = counts.at[:, :, 4].set(staying)
    incoming = incoming.at[:, :, 4].set(staying)
    send_keys = jax.random.split(subkeys[3], N_GX * N_GY)
    item_index = jax.vmap(lambda subkey: jax.random.permutation(subkey, SLOTS))(send_keys).reshape(N_GX, N_GY, SLOTS).astype(jnp.int32)
    recv_keys = jax.random.split(subkeys[4], N_GX * N_GY)
    placement = jax.vmap(lambda subkey: jax.random.permutation(subkey, SLOTS))(recv_keys).reshape(N_GX, N_GY, SLOTS).astype(jnp.int32)
    ends_cum = jnp.cumsum(counts, axis=-1)
    starts_cum = ends_cum - counts
    heading_code = jnp.sum((item_index[..., None] >= ends_cum[:, :, None, :]).astype(jnp.int32), axis=-1)
    clipped = jnp.minimum(heading_code, 8)
    lane_index = item_index - jnp.take_along_axis(starts_cum, clipped, axis=-1)
    is_live = heading_code < 9
    move_x = jnp.where(is_live, clipped // 3 - 1, 0)
    move_y = jnp.where(is_live, clipped % 3 - 1, 0)
    dest_x = jnp.clip(grid_x + move_x, 0, N_GX - 1)
    dest_y = jnp.clip(grid_y + move_y, 0, N_GY - 1)
    recv_starts = jnp.cumsum(incoming, axis=-1) - incoming
    recv_item = recv_starts[dest_x, dest_y, clipped] + lane_index
    target_slot = placement[dest_x, dest_y, jnp.clip(recv_item, 0, SLOTS - 1)]
    target_slot = jnp.where(is_live, target_slot, 0)
    return (heading_code, target_slot, dest_x, dest_y, move_x, move_y, subkeys[5])


def draw_move_codes(key, part):
    return bubble_plan(key)[0].astype(jnp.int32)


def draw_targets(key, part):
    return bubble_plan(key)[1].astype(jnp.int32)


def draw_positions(key, part):
    heading_code, target_slot, dest_x, dest_y, move_x, move_y, pos_key = bubble_plan(key)
    unit = jax.random.uniform(pos_key, (3, N_GX, N_GY, SLOTS), jnp.float32)
    near_x = min(4, CX)
    near_y = min(4, CY)
    local_x = jnp.where(move_x == 1, unit[0] * near_x, jnp.where(move_x == -1, CX - near_x * (1.0 - unit[0]), unit[0] * CX))
    local_y = jnp.where(move_y == 1, unit[1] * near_y, jnp.where(move_y == -1, CY - near_y * (1.0 - unit[1]), unit[1] * CY))
    coord_x = dest_x.astype(jnp.float32) * CX + local_x
    coord_y = dest_y.astype(jnp.float32) * CY + local_y
    coord_z = unit[2] * CZ
    return jnp.stack([coord_x, coord_y, coord_z]).astype(jnp.float32)


def steps_of(stream_key, dims, pieces, smallest, largest):
    def one(axis_at, shards_of):
        steps = jax.random.uniform(jax.random.fold_in(jax.random.fold_in(stream_key, 6), axis_at), (shards_of,), jnp.float32, smallest / len(pieces), largest / len(pieces))
        return jnp.repeat(jnp.exp(steps), dims[axis_at] // shards_of).reshape((-1,) + (1,) * (len(dims) - axis_at - 1))

    loudness = one(*pieces[0])
    for cut in pieces[1:]:
        loudness = loudness * one(*cut)
    return loudness


def scatter_about(key, dims, scale, most, shards=(), held_as=jnp.bfloat16):
    drawn = scale * jax.random.normal(key, dims, jnp.float32)
    if shards:
        drawn = drawn * steps_of(key, dims, shards, -0.22, 0.18)
    return jnp.clip(drawn, -most, most).astype(held_as)


def setup_inputs(seed: int = 0) -> dict:
    keys = jax.random.split(jax.random.key(seed), 11)
    fields = scatter_about(keys[0], (NF, CZ, NY, NX), 1.0, 4.0, ((2, 8), (3, 4)), jnp.float32)
    velocity = jnp.clip(jax.random.uniform(keys[1], (2, CZ, NY, NX), jnp.float32, -1.0, 1.0) * steps_of(keys[1], (2, CZ, NY, NX), ((2, 8), (3, 4)), -0.4, 0.0), -1.0, 1.0)
    coupling = jnp.clip(jnp.exp(jax.random.uniform(keys[2], (NF,), jnp.float32, math.log(0.5), math.log(4.0))), 0.5, 4.0)
    positions = draw_positions(jax.random.fold_in(keys[10], 71), 0)
    log_radius = jnp.clip(jax.random.uniform(keys[4], (N_GX, N_GY, SLOTS), jnp.float32, -0.35, 0.35) * steps_of(keys[4], (N_GX, N_GY, SLOTS), ((0, 4), (1, 8)), -0.4, 0.0), -0.35, 0.35)
    growth = jnp.clip(jax.random.uniform(keys[5], (N_GX, N_GY, SLOTS), jnp.float32, -0.5, 0.5) * steps_of(keys[5], (N_GX, N_GY, SLOTS), ((0, 4), (1, 8)), -0.4, 0.0), -0.5, 0.5)
    rest_gap = jnp.clip(jax.random.uniform(keys[6], (N_GX, N_GY, SLOTS), jnp.float32, -0.15, 0.15) * steps_of(keys[6], (N_GX, N_GY, SLOTS), ((0, 4), (1, 8)), -0.4, 0.0), -0.15, 0.15)
    gas_pressure = jnp.clip(jnp.exp(math.log(1.4) - 0.6931472 * jax.random.uniform(keys[7], (N_GX, N_GY, SLOTS), jnp.float32) ** steps_of(keys[7], (N_GX, N_GY, SLOTS), ((0, 4), (1, 8)), -0.2, 0.2)), 0.7, 1.4)
    move_codes = draw_move_codes(jax.random.fold_in(keys[10], 71), 0)
    targets = draw_targets(jax.random.fold_in(keys[10], 71), 0)
    return dict(fields=fields, velocity=velocity, coupling=coupling, positions=positions, log_radius=log_radius, growth=growth, rest_gap=rest_gap, gas_pressure=gas_pressure, move_codes=move_codes, targets=targets)


time_step = 0.2
weno_eps = 1e-6
four_pi = 4.0 * math.pi


def tent_weight(distance):
    return 0.5 * jnp.maximum(0.0, 1.0 - 0.5 * jnp.abs(distance))


def weno_side(first_val, second_val, third_val, fourth_val, fifth_val):
    left_poly = (2.0 * first_val - 7.0 * second_val + 11.0 * third_val) / 6.0
    mid_poly = (-second_val + 5.0 * third_val + 2.0 * fourth_val) / 6.0
    right_poly = (2.0 * third_val + 5.0 * fourth_val - fifth_val) / 6.0
    left_smooth = 13.0 / 12.0 * (first_val - 2.0 * second_val + third_val) ** 2 + 0.25 * (first_val - 4.0 * second_val + 3.0 * third_val) ** 2
    mid_smooth = 13.0 / 12.0 * (second_val - 2.0 * third_val + fourth_val) ** 2 + 0.25 * (second_val - fourth_val) ** 2
    right_smooth = 13.0 / 12.0 * (third_val - 2.0 * fourth_val + fifth_val) ** 2 + 0.25 * (3.0 * third_val - 4.0 * fourth_val + fifth_val) ** 2
    left_weight = 0.1 / (weno_eps + left_smooth) ** 2
    mid_weight = 0.6 / (weno_eps + mid_smooth) ** 2
    right_weight = 0.3 / (weno_eps + right_smooth) ** 2
    return (left_weight * left_poly + mid_weight * mid_poly + right_weight * right_poly) / (left_weight + mid_weight + right_weight)


def flux_div(values, speeds, axis_dim, length):
    def window(array, start):
        return lax.slice_in_dim(array, start, start + length + 1, axis=axis_dim)

    abs_speed = jnp.abs(speeds)
    split_speed = window(abs_speed, 0)
    for offset in range(1, 6):
        split_speed = jnp.maximum(split_speed, window(abs_speed, offset))
    flux_cells = speeds * values
    right_moving = [0.5 * (window(flux_cells, offset) + split_speed * window(values, offset)) for offset in range(5)]
    left_moving = [0.5 * (window(flux_cells, offset) - split_speed * window(values, offset)) for offset in range(1, 6)]
    face_flux = weno_side(*right_moving) + weno_side(left_moving[4], left_moving[3], left_moving[2], left_moving[1], left_moving[0])
    return lax.slice_in_dim(face_flux, 1, length + 1, axis=axis_dim) - lax.slice_in_dim(face_flux, 0, length, axis=axis_dim)


def reference(fields, velocity, coupling, positions, log_radius, growth, rest_gap, gas_pressure, move_codes, targets):
    all_slots = N_GX * N_GY * SLOTS
    grid_x = jnp.arange(N_GX, dtype=jnp.int32)[:, None, None]
    grid_y = jnp.arange(N_GY, dtype=jnp.int32)[None, :, None]
    destination = ((grid_x + move_codes // 3 - 1) * N_GY + (grid_y + move_codes % 3 - 1)) * SLOTS + targets
    destination = jnp.where(move_codes < 9, destination, all_slots).reshape(-1).astype(jnp.int32)
    packed = jnp.stack([positions[0], positions[1], positions[2], log_radius, growth, rest_gap, gas_pressure]).reshape(7, all_slots)
    rehomed = jnp.zeros((7, all_slots), fields.dtype).at[:, destination].set(packed, mode="drop")
    occupied = jnp.zeros((all_slots,), fields.dtype).at[destination].set(1.0, mode="drop")
    pos_x, pos_y, pos_z = rehomed[0], rehomed[1], rehomed[2]
    offsets = jnp.arange(-1, 3, dtype=jnp.int32)
    cell_x = jnp.floor(pos_x - 0.5).astype(jnp.int32)[:, None] + offsets
    cell_y = jnp.floor(pos_y - 0.5).astype(jnp.int32)[:, None] + offsets
    cell_z = jnp.floor(pos_z - 0.5).astype(jnp.int32)[:, None] + offsets
    weight_x = tent_weight(pos_x[:, None] - (cell_x.astype(pos_x.dtype) + 0.5))
    weight_y = tent_weight(pos_y[:, None] - (cell_y.astype(pos_y.dtype) + 0.5))
    weight_z = tent_weight(pos_z[:, None] - (cell_z.astype(pos_z.dtype) + 0.5))
    kernel = weight_z[:, :, None, None] * weight_y[:, None, :, None] * weight_x[:, None, None, :]
    index_z = jnp.mod(cell_z, CZ)[:, :, None, None]
    index_y = cell_y[:, None, :, None] + 2
    index_x = cell_x[:, None, None, :] + 2

    def sample(first_field):
        padded = jnp.pad(first_field, ((0, 0), (2, 2), (2, 2)))
        return jnp.sum(kernel * padded[index_z, index_y, index_x], axis=(1, 2, 3))

    def smear_sum(volume):
        grid = jnp.zeros((CZ, NY + 4, NX + 4), fields.dtype)
        grid = grid.at[index_z, index_y, index_x].add(kernel * volume[:, None, None, None])
        return grid[:, 2:-2, 2:-2]

    velocity_pad = jnp.pad(velocity, ((0, 0), (0, 0), (3, 3), (3, 3)))

    def gas_rate(gas_state, source):
        state_pad = jnp.pad(gas_state, ((0, 0), (0, 0), (3, 3), (3, 3)))

        def plane_rate(pair):
            state_plane, flow_plane = pair
            div_x = flux_div(state_plane[:, 3:-3, :], flow_plane[0][None, 3:-3, :], 2, NX)
            div_y = flux_div(state_plane[:, :, 3:-3], flow_plane[1][None, :, 3:-3], 1, NY)
            return div_x + div_y

        divergence = lax.map(plane_rate, (state_pad.transpose(1, 0, 2, 3), velocity_pad.transpose(1, 0, 2, 3)))
        return -divergence.transpose(1, 0, 2, 3) + coupling[:, None, None, None] * source[None]

    rest_log = rehomed[3] + rehomed[5]
    pressure_gas = rehomed[6]

    def rates(radius_log, radius_rate, gas_state):
        sampled = sample(gas_state[0])
        pressure_gap = pressure_gas * jnp.exp(-3.0 * (radius_log - rest_log)) - 1.0 - 0.5 * sampled - 0.2 * radius_rate
        rate_w = pressure_gap * jnp.exp(-2.0 * radius_log) - 2.5 * radius_rate * radius_rate
        smeared = smear_sum(occupied * four_pi * jnp.exp(3.0 * radius_log) * radius_rate)
        return radius_rate, rate_w, gas_rate(gas_state, smeared)

    radius_zero, rate_zero = rehomed[3], rehomed[4]
    rate_s, rate_w, change = rates(radius_zero, rate_zero, fields)
    fields_one = fields + time_step * change
    radius_one = radius_zero + time_step * rate_s
    rate_one = rate_zero + time_step * rate_w
    rate_s, rate_w, change = rates(radius_one, rate_one, fields_one)
    new_fields = 0.5 * fields + 0.5 * (fields_one + time_step * change)
    radius_two = 0.5 * radius_zero + 0.5 * (radius_one + time_step * rate_s)
    rate_two = 0.5 * rate_zero + 0.5 * (rate_one + time_step * rate_w)
    new_bubbles = jnp.stack([radius_two * occupied, rate_two * occupied]).reshape(2, N_GX, N_GY, SLOTS)
    return new_fields, new_bubbles
```

```python
import functools
import math

import jax
import jax.numpy as jnp
from jax import lax
from jax.experimental import pallas as pl
from jax.experimental.pallas import tpu as pltpu
from jax.sharding import PartitionSpec as P

time_step = 0.2
four_pi = 4.0 * math.pi
speed_scale = 1.0 / 16.0
smooth_eps = 3e-6 * speed_scale * speed_scale
flux_unit = 1.0 / (12.0 * speed_scale)

DIRS = [c for c in range(9) if c != 4]
X_DIRS = (1, 7)
Y_DIRS = (3, 5)
DIAG = (0, 2, 6, 8)


def weno_offset(d1, d2, d3, d4):
    t1 = d2 - d1
    t2 = d3 - d2
    t3 = d4 - d3
    d2q = 0.75 * d2
    d3q = 0.75 * d3
    b0 = t1 * t1 + (d2q * (t1 + d2) + smooth_eps)
    b1 = t2 * t2 + (d2q * d3 + smooth_eps)
    b2 = t3 * t3 + (d3q * (d3 - t3) + smooth_eps)
    m0 = b1 * b2
    m1 = b0 * b2
    m2 = b0 * b1
    w0 = m0 * m0
    w1 = 6.0 * (m1 * m1)
    w2 = 3.0 * (m2 * m2)
    a = t1 - t2
    return (w0 * (a + a) + w2 * (t2 - t3)) / (w0 + w1 + w2)


def face_flux(q, u):
    up, down = u
    g = [up[i] * q[i] for i in range(5)]
    h = [down[i] * q[i + 1] for i in range(5)]
    r = [g[i + 1] - g[i] for i in range(4)]
    l = [h[i + 1] - h[i] for i in range(4)]
    mid = r[2] - l[1]
    line = 6.0 * (g[2] + h[2]) + ((r[1] - l[2]) + (mid + mid))
    return line + (weno_offset(*r) - weno_offset(l[3], l[2], l[1], l[0]))


def split_max(u):
    a = [jnp.abs(v) for v in u]
    top = jnp.maximum(
        jnp.maximum(jnp.maximum(a[0], a[1]), jnp.maximum(a[2], a[3])), jnp.maximum(a[4], a[5])
    )
    return [v + top for v in u[:5]], [v - top for v in u[1:]]


def split2(v):
    hi = v.astype(jnp.bfloat16)
    lo = (v - hi.astype(jnp.float32)).astype(jnp.bfloat16)
    return hi, lo


def split3_rows(v):
    hi = v.astype(jnp.bfloat16).astype(jnp.float32)
    rest = v - hi
    mid = rest.astype(jnp.bfloat16).astype(jnp.float32)
    return jnp.concatenate([hi, mid, rest - mid], axis=0)


def tent(d):
    return 0.5 * jnp.maximum(0.0, 1.0 - 0.5 * jnp.abs(d))


def dot(a, b, trans):
    dims = (((1,), (1,)), ((), ())) if trans else (((1,), (0,)), ((), ()))
    return lax.dot_general(a, b, dims, preferred_element_type=jnp.float32)


def kernel(
    n_gx,
    n_gy,
    dims,
    fields_ref,
    vel_ref,
    coup_hbm,
    pos_hbm,
    lr_hbm,
    gr_hbm,
    rg_hbm,
    gp_hbm,
    code_hbm,
    tgt_hbm,
    out_ref,
    bub_ref,
    coup_ref,
    pos_ref,
    lr_ref,
    gr_ref,
    rg_ref,
    gp_ref,
    code_ref,
    tgt_ref,
    small_sem,
    q,
    q1,
    ux,
    s_own,
    s_in,
    c_in,
    s1_own,
    s1_in,
    c1_in,
    outbox,
    inbox,
    vals,
    samp,
    wxh,
    wxl,
    wzy,
    dep,
    depx,
    depc,
    dy_in,
    dx_in,
    dc_in,
    smear,
    eface,
    yface,
    drim,
    stage,
    acc,
    in_sem,
    out_sem,
    send_sem,
    recv_sem,
):
    nf, nz, ny, nx, slots = dims
    f32 = jnp.float32
    me_x = lax.axis_index("gx")
    me_y = lax.axis_index("gy")
    lane = lax.broadcasted_iota(jnp.int32, (nz, nx), 1)
    group = lane // 8
    sub = lane % 8

    def inside(c, sign):
        a, b = sign * (c // 3 - 1), sign * (c % 3 - 1)
        ok = None
        for pos, step, count in ((me_x, a, n_gx), (me_y, b, n_gy)):
            cond = None
            if step == 1:
                cond = pos < count - 1
            elif step == -1:
                cond = pos > 0
            if cond is not None:
                ok = cond if ok is None else jnp.logical_and(ok, cond)
        return ok

    def desc(kind, c, src, dst):
        return pltpu.make_async_remote_copy(
            src_ref=src,
            dst_ref=dst,
            send_sem=send_sem.at[kind, c],
            recv_sem=recv_sem.at[kind, c],
            device_id=(me_x + (c // 3 - 1), me_y + (c % 3 - 1)),
            device_id_type=pl.DeviceIdType.MESH,
        )

    def send(kind, c, src, dst):
        @pl.when(inside(c, 1))
        def _():
            desc(kind, c, src, dst).start()

    def sent(kind, c, src, dst):
        @pl.when(inside(c, 1))
        def _():
            desc(kind, c, src, dst).wait_send()

    def recv(kind, c, src, dst):
        @pl.when(inside(c, -1))
        def _():
            desc(kind, c, src, dst).wait_recv()

        @pl.when(jnp.logical_not(inside(c, -1)))
        def _():
            dst[...] = jnp.zeros(dst.shape, f32)

    def rim_msgs(buf, packed, packed_in, corner_in):
        count = packed.shape[0]
        depth = buf.shape[0]
        yield 3, buf.at[:, pl.ds(3, 3)], buf.at[:, pl.ds(ny + 3, 3)]
        yield 5, buf.at[:, pl.ds(ny, 3)], buf.at[:, pl.ds(0, 3)]
        for n, c in enumerate(X_DIRS):
            yield c, packed, packed_in.at[n]
        for n, c in enumerate(DIAG):
            yield c, packed.at[0], corner_in.at[n]

    def smear_msgs(s):
        yield 3, dep.at[s, pl.ds(0, 2)], dy_in.at[s, 0]
        yield 5, dep.at[s, pl.ds(ny + 2, 2)], dy_in.at[s, 1]
        for n, c in enumerate(X_DIRS):
            yield c, depx.at[s], dx_in.at[s, n]
        for n, c in enumerate(DIAG):
            yield c, depc.at[s], dc_in.at[s, n]

    bubble_msgs = [(c, outbox.at[n], inbox.at[n]) for n, c in enumerate(DIRS)]
    rims0 = list(rim_msgs(q, s_own, s_in, c_in))
    rims1 = list(rim_msgs(q1, s1_own, s1_in, c1_in))
    smears = [list(smear_msgs(0)), list(smear_msgs(1))]

    small = [
        pltpu.make_async_copy(src, dst, small_sem.at[n])
        for n, (src, dst) in enumerate(
            (
                (code_hbm, code_ref),
                (tgt_hbm, tgt_ref),
                (pos_hbm, pos_ref),
                (lr_hbm, lr_ref),
                (gr_hbm, gr_ref),
                (rg_hbm, rg_ref),
                (gp_hbm, gp_ref),
                (coup_hbm, coup_ref),
            )
        )
    ]
    for copy in small:
        copy.start()
    loads = []
    for y in range(ny):
        loads.append(
            pltpu.make_async_copy(
                fields_ref.at[:, :, y, :], q.at[pl.ds(0, nf), y + 3], in_sem.at[3 * y]
            )
        )
        loads.append(
            pltpu.make_async_copy(vel_ref.at[1, :, y, :], q.at[nf, y + 3], in_sem.at[3 * y + 1])
        )
        loads.append(
            pltpu.make_async_copy(vel_ref.at[0, :, y, :], ux.at[y], in_sem.at[3 * y + 2])
        )
    for copy in loads:
        copy.start()

    barrier = pltpu.get_barrier_semaphore()
    neighbours = jnp.int32(0)
    for c in DIRS:
        ok = inside(c, 1)

        @pl.when(ok)
        def _():
            pl.semaphore_signal(
                barrier,
                inc=1,
                device_id=(me_x + (c // 3 - 1), me_y + (c % 3 - 1)),
                device_id_type=pl.DeviceIdType.MESH,
            )

        neighbours = neighbours + ok.astype(jnp.int32)

    for copy in small:
        copy.wait()
    code = code_ref[0]
    target = tgt_ref[0]
    for r in range(3):
        vals[pl.ds(r, 1), :] = pos_ref[r, 0]
    vals[pl.ds(3, 1), :] = lr_ref[0]
    vals[pl.ds(4, 1), :] = gr_ref[0]
    vals[pl.ds(5, 1), :] = rg_ref[0]
    vals[pl.ds(6, 1), :] = gp_ref[0]
    vals[pl.ds(7, 1), :] = (target + 1).astype(f32)
    parts = split3_rows(vals[...])
    row16 = lax.broadcasted_iota(jnp.int32, (16, slots), 0)
    moves = jnp.where((row16 == code) & (row16 != 4) & (row16 < 9), 1.0, 0.0).astype(f32)
    chunks = slots // 128
    stacked = jnp.concatenate(
        [moves[:, 128 * k : 128 * (k + 1)] for k in range(chunks)], axis=0
    )
    upper = lax.broadcasted_iota(jnp.int32, (128, 128), 0) < lax.broadcasted_iota(
        jnp.int32, (128, 128), 1
    )
    before = dot(
        stacked.astype(jnp.bfloat16), jnp.where(upper, 1.0, 0.0).astype(jnp.bfloat16), False
    )
    offset = jnp.zeros((16, 1), f32)
    ranks = []
    for k in range(chunks):
        chunk = stacked[16 * k : 16 * (k + 1)]
        ranks.append(
            jnp.sum(chunk * (before[16 * k : 16 * (k + 1)] + offset), axis=0, keepdims=True)
        )
        offset = offset + jnp.sum(chunk, axis=1, keepdims=True)
    rank = jnp.concatenate(ranks, axis=1)
    row128 = lax.broadcasted_iota(jnp.int32, (128, slots), 0)
    pick = jnp.where(row128.astype(f32) == rank, 1.0, 0.0).astype(jnp.bfloat16)
    masked = jnp.concatenate([jnp.where(code == c, parts, 0.0) for c in DIRS], axis=0)
    boxes = dot(masked.astype(jnp.bfloat16), pick, True)
    for n in range(8):
        outbox[n] = (
            boxes[24 * n : 24 * n + 8] + boxes[24 * n + 8 : 24 * n + 16]
        ) + boxes[24 * n + 16 : 24 * n + 24]

    pl.semaphore_wait(barrier, neighbours)
    for c, src, dst in bubble_msgs:
        send(0, c, src, dst)

    for copy in loads:
        copy.wait()

    def pack_rows(rows):
        packed = jnp.zeros((nz, nx), f32)
        for y, row in rows:
            packed = jnp.where(group == y, pltpu.roll(row, (8 * y + 3) % nx, 1), packed)
        return packed

    for c, src, dst in rims0[:2]:
        send(1, c, src, dst)
    for f in range(nf):
        s_own[f] = pack_rows([(y, q[f, y + 3]) for y in range(ny)])
    s_own[nf] = pack_rows([(y, ux[y]) for y in range(ny)])
    for c, src, dst in rims0[2:]:
        send(1, c, src, dst)

    def y_faces(buf, first, count, skip):
        def body(k, carry):
            y = first + k + jnp.where(k >= 3, skip, 0)
            u = split_max([speed_scale * q[nf, y + 1 + o] for o in range(6)])
            for f in range(nf):
                yface[f, y + 1] = face_flux([buf[f, y + 1 + o] for o in range(6)], u)
            return carry

        lax.fori_loop(0, count, body, 0)

    def inner_faces(buf):
        y_faces(buf, 2, ny - 5, 0)

    def outer_faces(buf):
        y_faces(buf, -1, 6, ny - 5)

    inner_faces(q)

    for c, src, dst in bubble_msgs:
        recv(0, c, src, dst)
    stay = jnp.where(code == 4, vals[...], 0.0)
    all_vals = jnp.concatenate([stay] + [inbox[n] for n in range(8)], axis=1)
    slot = all_vals[7:8].astype(jnp.int32) - 1
    slot_hi = slot >> 7
    slot_lo = slot & 127
    total = all_vals.shape[1]
    place = jnp.where(
        lax.broadcasted_iota(jnp.int32, (128, total), 0) == slot_lo, 1.0, 0.0
    ).astype(jnp.bfloat16)
    all_parts = split3_rows(all_vals)
    spread = jnp.concatenate(
        [jnp.where(slot_hi == h, all_parts, 0.0) for h in range(chunks)], axis=0
    )
    homes = dot(spread.astype(jnp.bfloat16), place, True)
    bubbles = jnp.concatenate(
        [
            (homes[24 * h : 24 * h + 8] + homes[24 * h + 8 : 24 * h + 16])
            + homes[24 * h + 16 : 24 * h + 24]
            for h in range(chunks)
        ],
        axis=1,
    )
    occupied = jnp.where(bubbles[7:8] > 0.5, 1.0, 0.0)
    local_x = bubbles[0:1] - (me_x * nx).astype(f32)
    local_y = bubbles[1:2] - (me_y * ny).astype(f32)
    cell = lax.broadcasted_iota(jnp.int32, (nx, slots), 0)
    rim_cell = jnp.where(cell < nx // 2, cell + nx, cell - nx)
    hi, lo = split2(tent(local_x - (cell.astype(f32) + 0.5)))
    wxh[pl.ds(0, nx)] = hi
    wxl[pl.ds(0, nx)] = lo
    hi, lo = split2(tent(local_x - (rim_cell.astype(f32) + 0.5)))
    wxh[pl.ds(nx, nx)] = hi
    wxl[pl.ds(nx, nx)] = lo
    z_dist = jnp.abs(
        bubbles[2:3] - (lax.broadcasted_iota(jnp.int32, (nz, slots), 0).astype(f32) + 0.5)
    )
    weight_z = tent(jnp.minimum(z_dist, nz - z_dist))
    for ye in range(ny + 4):
        wzy[pl.ds(ye * nz, nz)] = weight_z * tent(local_y - (ye - 1.5))

    rows = (ny + 4) * nz
    step_rows = rows // 4

    def sample_rows(start, count):
        ph, plow = split2(samp[pl.ds(start, count)])
        both = dot(jnp.concatenate([ph, plow], axis=0), wxh[...], False)
        table = both[:count] + both[count:] + dot(ph, wxl[...], False)
        prod = table * wzy[pl.ds(start, count)]
        part = prod[0:8]
        for k in range(1, count // 8):
            part = part + prod[8 * k : 8 * (k + 1)]
        acc[...] += part

    def sampled_rest():
        sample_rows(ny * nz, 4 * nz)
        return jnp.sum(acc[...], axis=0, keepdims=True)

    def deposit(s, volume):
        planes = step_rows // nz

        def body(k, carry):
            part = wzy[pl.ds(pl.multiple_of(k * step_rows, step_rows), step_rows)] * volume
            ph, plow = split2(part)
            both = dot(jnp.concatenate([ph, plow], axis=0), wxh[...], True)
            d = both[:step_rows] + both[step_rows:] + dot(ph, wxl[...], True)
            for r in range(planes):
                dep[s, k * planes + r] = d[r * nz : (r + 1) * nz, :nx]
                drim[k * planes + r] = d[r * nz : (r + 1) * nz, nx:]
            return carry

        lax.fori_loop(0, 4, body, 0)
        rims = [drim[r] for r in range(ny + 4)]
        depx[s] = pack_rows([(y, rims[y + 2]) for y in range(ny)])
        depc[s] = pack_rows(
            [(0, rims[ny + 2]), (1, rims[ny + 3]), (ny - 2, rims[0]), (ny - 1, rims[1])]
        )
        for c, src, dst in smears[s]:
            send(2 + s, c, src, dst)

    def gather_smear(s):
        for c, src, dst in smears[s]:
            recv(2 + s, c, src, dst)
        low = lane < nx // 2
        from_right = dx_in[s, 0] + jnp.where(low, dc_in[s, 1], dc_in[s, 0])
        from_left = dx_in[s, 1] + jnp.where(low, dc_in[s, 3], dc_in[s, 2])
        merged = jnp.where(sub >= 3, from_left, from_right)
        edge = (lane < 2) | (lane >= nx - 2)
        for y in range(ny):
            total_row = dep[s, y + 2] + jnp.where(
                edge, pltpu.roll(merged, (nx - 8 * y - 3) % nx, 1), 0.0
            )
            if y < 2:
                total_row = total_row + dy_in[s, 1, y]
            if y >= ny - 2:
                total_row = total_row + dy_in[s, 0, y - (ny - 2)]
            smear[y] = total_row

    def fill_sample(buf, own, got, corner):
        left = sub < 3
        mid = jnp.where(left, got[1, 0], got[0, 0])
        top = jnp.where(left, corner[3], corner[1])
        bottom = jnp.where(left, corner[2], corner[0])
        for ye in range(ny + 4):
            y = ye - 2
            samp[pl.ds(ye * nz, nz), pl.ds(0, nx)] = buf[0, ye + 1]
            source = top if y < 0 else (bottom if y >= ny else mid)
            home = y + ny if y < 0 else (y - ny if y >= ny else y)
            samp[pl.ds(ye * nz, nz), pl.ds(nx, nx)] = pltpu.roll(
                source, (nx - 8 * home - 3) % nx, 1
            )

    rest_log = bubbles[3:4] + bubbles[5:6]
    pressure_gas = bubbles[6:7]

    def rate_of(s, w, sampled):
        gap = (
            pressure_gas * jnp.exp(-3.0 * (s - rest_log)) - 1.0 - 0.5 * sampled - 0.2 * w
        )
        return gap * jnp.exp(-2.0 * s) - 2.5 * w * w

    def volume_of(s, w):
        return occupied * four_pi * jnp.exp(3.0 * s) * w

    s_zero, w_zero = bubbles[3:4], bubbles[4:5]
    deposit(0, volume_of(s_zero, w_zero))
    def x_windows(x, r):
        return [
            pltpu.roll(jnp.where(lane >= nx - 2, r, x), 2, 1),
            pltpu.roll(jnp.where(lane >= nx - 1, r, x), 1, 1),
            x,
            pltpu.roll(jnp.where(lane < 1, r, x), nx - 1, 1),
            pltpu.roll(jnp.where(lane < 2, r, x), nx - 2, 1),
            pltpu.roll(jnp.where(lane < 3, r, x), nx - 3, 1),
        ]

    def packed_windows(p):
        return [p] + [pltpu.roll(p, nx - o, 1) for o in range(1, 6)]

    def divergence(buf, own, got, emit):
        left = sub < 3
        ue = split_max(packed_windows(speed_scale * jnp.where(left, s_in[1, nf], s_own[nf])))
        for f in range(nf):
            e = face_flux(packed_windows(jnp.where(left, got[1, f], own[f])), ue)
            eface[f] = pltpu.roll(e, 3, 1)
        acc[...] = jnp.zeros((8, slots), f32)

        def body(y, carry):
            sample_rows(pl.multiple_of(y * nz, nz), nz)
            shift = (nx - 3) - 8 * y
            ur = pltpu.roll(jnp.where(left, s_in[1, nf], s_in[0, nf]), shift, 1)
            uxw = split_max([speed_scale * v for v in x_windows(ux[y], ur)])
            for f in range(nf):
                r = pltpu.roll(jnp.where(left, got[1, f], got[0, f]), shift, 1)
                fx = face_flux(x_windows(buf[f, y + 3], r), uxw)
                fx_before = jnp.where(
                    lane == 0, pltpu.roll(eface[f], shift, 1), pltpu.roll(fx, 1, 1)
                )
                emit(f, y, (fx - fx_before) + (yface[f, y + 1] - yface[f, y]))
            return carry

        lax.fori_loop(0, ny, body, 0)

    for c, src, dst in rims0:
        recv(1, c, src, dst)
    fill_sample(q, s_own, s_in, c_in)
    outer_faces(q)

    def emit_one(f, y, div):
        q1[f, y + 3] = q[f, y + 3] - (time_step * flux_unit) * div

    divergence(q, s_own, s_in, emit_one)
    gather_smear(0)
    for y in range(ny):
        source = time_step * smear[y]
        for f in range(nf):
            q1[f, y + 3] = q1[f, y + 3] + coup_ref[f] * source
    for c, src, dst in rims1[:2]:
        send(4, c, src, dst)
    for f in range(nf):
        s1_own[f] = pack_rows([(y, q1[f, y + 3]) for y in range(ny)])
    for c, src, dst in rims1[2:]:
        send(4, c, src, dst)

    s_one = s_zero + time_step * w_zero
    w_one = w_zero + time_step * rate_of(s_zero, w_zero, sampled_rest())
    deposit(1, volume_of(s_one, w_one))
    inner_faces(q1)
    for c, src, dst in rims1:
        recv(4, c, src, dst)
    fill_sample(q1, s1_own, s1_in, c1_in)
    outer_faces(q1)

    def emit_two(f, y, div):
        stage[f, y] = 0.5 * (q[f, y + 3] + q1[f, y + 3]) - (0.5 * time_step * flux_unit) * div

    divergence(q1, s1_own, s1_in, emit_two)
    gather_smear(1)
    stores = []
    for y in range(ny):
        source = (0.5 * time_step) * smear[y]
        for f in range(nf):
            stage[f, y] = stage[f, y] + coup_ref[f] * source
        stores.append(
            pltpu.make_async_copy(stage.at[:, y], out_ref.at[:, :, y, :], out_sem.at[y])
        )
        stores[y].start()
    rate_two = rate_of(s_one, w_one, sampled_rest())
    s_two = 0.5 * s_zero + 0.5 * (s_one + time_step * w_one)
    w_two = 0.5 * w_zero + 0.5 * (w_one + time_step * rate_two)
    bub_ref[0, 0] = s_two * occupied
    bub_ref[1, 0] = w_two * occupied
    for copy in stores:
        copy.wait()

    for kind, msgs in ((0, bubble_msgs), (1, rims0), (2, smears[0]), (3, smears[1]), (4, rims1)):
        for c, src, dst in msgs:
            sent(kind, c, src, dst)


def shards(n_gx, n_gy, fields, velocity, coupling, positions, log_radius, growth, rest_gap,
           gas_pressure, move_codes, targets):
    nf, nz, ny, nx = fields.shape
    slots = move_codes.shape[2]
    vmem = pl.BlockSpec(memory_space=pltpu.VMEM)
    f32 = jnp.float32
    rows = (ny + 4) * nz
    sc = lambda *shape: pltpu.VMEM(shape, f32)
    out, bub = pl.pallas_call(
        functools.partial(kernel, n_gx, n_gy, (nf, nz, ny, nx, slots)),
        out_shape=(
            pltpu.VMEM((nf, nz, ny, nx), f32),
            pltpu.VMEM((2, 1, 1, slots), f32),
        ),
        in_specs=[pl.BlockSpec(memory_space=pltpu.HBM)] * 10,
        out_specs=(vmem, vmem),
        scratch_shapes=[
            pltpu.SMEM((nf,), f32),
            sc(3, 1, 1, slots),
            sc(1, 1, slots),
            sc(1, 1, slots),
            sc(1, 1, slots),
            sc(1, 1, slots),
            pltpu.VMEM((1, 1, slots), jnp.int32),
            pltpu.VMEM((1, 1, slots), jnp.int32),
            pltpu.SemaphoreType.DMA((8,)),
            sc(nf + 1, ny + 6, nz, nx),
            sc(nf, ny + 6, nz, nx),
            sc(ny, nz, nx),
            sc(nf + 1, nz, nx),
            sc(2, nf + 1, nz, nx),
            sc(4, nz, nx),
            sc(nf, nz, nx),
            sc(2, nf, nz, nx),
            sc(4, nz, nx),
            sc(8, 8, 128),
            sc(8, 8, 128),
            sc(8, slots),
            sc(rows, 2 * nx),
            pltpu.VMEM((2 * nx, slots), jnp.bfloat16),
            pltpu.VMEM((2 * nx, slots), jnp.bfloat16),
            sc(rows, slots),
            sc(2, ny + 4, nz, nx),
            sc(2, nz, nx),
            sc(2, nz, nx),
            sc(2, 2, 2, nz, nx),
            sc(2, 2, nz, nx),
            sc(2, 4, nz, nx),
            sc(ny, nz, nx),
            sc(nf, nz, nx),
            sc(nf, ny + 1, nz, nx),
            sc(ny + 4, nz, nx),
            sc(nf, ny, nz, nx),
            sc(8, slots),
            pltpu.SemaphoreType.DMA((3 * ny,)),
            pltpu.SemaphoreType.DMA((ny,)),
            pltpu.SemaphoreType.DMA((5, 9)),
            pltpu.SemaphoreType.DMA((5, 9)),
        ],
        compiler_params=pltpu.CompilerParams(
            collective_id=0, has_side_effects=True
        ),
    )(fields, velocity, coupling, positions, log_radius, growth, rest_gap, gas_pressure,
      move_codes, targets)
    return out, bub


def solution(mesh):
    placed = (
        P(None, None, "gy", "gx"),
        P(None, None, "gy", "gx"),
        P(),
        P(None, "gx", "gy", None),
        P("gx", "gy", None),
        P("gx", "gy", None),
        P("gx", "gy", None),
        P("gx", "gy", None),
        P("gx", "gy", None),
        P("gx", "gy", None),
    )
    return jax.shard_map(
        functools.partial(shards, mesh.shape["gx"], mesh.shape["gy"]),
        mesh=mesh,
        in_specs=placed,
        out_specs=(P(None, None, "gy", "gx"), P(None, "gx", "gy", None)),
        check_vma=False,
    )
```

```python
import functools
import math

import jax
import jax.numpy as jnp
from jax import lax
from jax.experimental import pallas as pl
from jax.experimental.pallas import tpu as pltpu
from jax.sharding import PartitionSpec as P

time_step = 0.2
four_pi = 4.0 * math.pi
smooth_eps = 3e-6
flux_unit = 1.0 / 12.0

DIRS = [c for c in range(9) if c != 4]
X_DIRS = (1, 7)
Y_DIRS = (3, 5)
DIAG = (0, 2, 6, 8)


def weno_side(d1, d2, d3, d4):
    t1 = d2 - d1
    t2 = d3 - d2
    t3 = d4 - d3
    x = 0.75 * d2
    y = 0.75 * d3
    b0 = t1 * (t1 + x) + (x * d2 + smooth_eps)
    b1 = t2 * t2 + (x * d3 + smooth_eps)
    b2 = t3 * (t3 - y) + (y * d3 + smooth_eps)
    j1 = b0 / b1
    j2 = b0 / b2
    w2 = (1.5 * j2) * j2
    w1 = (3.0 * j1) * j1
    return ((t1 - t2) + w2 * (t2 - t3)) / (w2 + w1 + 0.5) - t2


def face_flux(dq, df, pair, top):
    p = [top * d for d in dq]
    r = [df[i] + p[i] for i in range(4)]
    l = [df[i + 1] - p[i + 1] for i in range(4)]
    return 6.0 * pair + (weno_side(*r) - weno_side(l[3], l[2], l[1], l[0]))


def split_max(u):
    a = [jnp.abs(v) for v in u]
    return jnp.maximum(
        jnp.maximum(jnp.maximum(a[0], a[1]), jnp.maximum(a[2], a[3])), jnp.maximum(a[4], a[5])
    )


def split2(v):
    hi = v.astype(jnp.bfloat16)
    lo = (v - hi.astype(jnp.float32)).astype(jnp.bfloat16)
    return hi, lo


def split3_rows(v):
    hi = v.astype(jnp.bfloat16).astype(jnp.float32)
    rest = v - hi
    mid = rest.astype(jnp.bfloat16).astype(jnp.float32)
    return jnp.concatenate([hi, mid, rest - mid], axis=0)


def tent(d):
    return jnp.maximum(0.0, 0.5 - jnp.abs(0.25 * d))


def dot(a, b, trans):
    dims = (((1,), (1,)), ((), ())) if trans else (((1,), (0,)), ((), ()))
    return lax.dot_general(a, b, dims, preferred_element_type=jnp.float32)


def kernel(
    n_gx,
    n_gy,
    dims,
    fields_ref,
    vel_ref,
    coup_hbm,
    pos_hbm,
    lr_hbm,
    gr_hbm,
    rg_hbm,
    gp_hbm,
    code_hbm,
    tgt_hbm,
    out_ref,
    bub_ref,
    coup_ref,
    pos_ref,
    lr_ref,
    gr_ref,
    rg_ref,
    gp_ref,
    code_ref,
    tgt_ref,
    small_sem,
    q,
    q1,
    ux,
    qt,
    qt1,
    topy,
    topx,
    dq_s,
    df_s,
    pair_s,
    xface,
    dv,
    pk,
    pk_in,
    c_in,
    pk1,
    pk1_in,
    c1_in,
    tb,
    outbox,
    inbox,
    vals,
    samp,
    wx,
    wzy,
    part_s,
    dep,
    depx,
    depc,
    dy_in,
    dx_in,
    dc_in,
    smear,
    yface,
    drim,
    stage,
    in_sem,
    out_sem,
    send_sem,
    recv_sem,
):
    nf, nz, ny, nx, slots = dims
    f32 = jnp.float32
    me_x = lax.axis_index("gx")
    me_y = lax.axis_index("gy")
    lane = lax.broadcasted_iota(jnp.int32, (nz, nx), 1)
    group = lane // 8
    sub = lane % 8

    def inside(c, sign):
        a, b = sign * (c // 3 - 1), sign * (c % 3 - 1)
        ok = None
        for pos, step, count in ((me_x, a, n_gx), (me_y, b, n_gy)):
            cond = None
            if step == 1:
                cond = pos < count - 1
            elif step == -1:
                cond = pos > 0
            if cond is not None:
                ok = cond if ok is None else jnp.logical_and(ok, cond)
        return ok

    def desc(kind, c, src, dst):
        return pltpu.make_async_remote_copy(
            src_ref=src,
            dst_ref=dst,
            send_sem=send_sem.at[kind, c],
            recv_sem=recv_sem.at[kind, c],
            device_id=(me_x + (c // 3 - 1), me_y + (c % 3 - 1)),
            device_id_type=pl.DeviceIdType.MESH,
        )

    def send(kind, c, src, dst):
        @pl.when(inside(c, 1))
        def _():
            desc(kind, c, src, dst).start()

    def sent(kind, c, src, dst):
        @pl.when(inside(c, 1))
        def _():
            desc(kind, c, src, dst).wait_send()

    def recv(kind, c, src, dst):
        @pl.when(inside(c, -1))
        def _():
            desc(kind, c, src, dst).wait_recv()

        @pl.when(jnp.logical_not(inside(c, -1)))
        def _():
            dst[...] = jnp.zeros(dst.shape, f32)

    def rim_msgs(buf, packed, packed_in, corner_in):
        yield 3, buf.at[:, pl.ds(3, 3)], buf.at[:, pl.ds(ny + 3, 3)]
        yield 5, buf.at[:, pl.ds(ny, 3)], buf.at[:, pl.ds(0, 3)]
        for n, c in enumerate(X_DIRS):
            yield c, packed.at[n], packed_in.at[n]
        for n, c in enumerate(DIAG):
            yield c, packed.at[n // 2, pl.ds(0, 8)], corner_in.at[n]

    def smear_msgs(s):
        yield 3, dep.at[s, pl.ds(0, 2)], dy_in.at[s, 0]
        yield 5, dep.at[s, pl.ds(ny + 2, 2)], dy_in.at[s, 1]
        for n, c in enumerate(X_DIRS):
            yield c, depx.at[s], dx_in.at[s, n]
        for n, c in enumerate(DIAG):
            yield c, depc.at[s], dc_in.at[s, n]

    bubble_msgs = [(c, outbox.at[n], inbox.at[n]) for n, c in enumerate(DIRS)]
    rims0 = list(rim_msgs(q, pk, pk_in, c_in))
    rims1 = list(rim_msgs(q1, pk1, pk1_in, c1_in))
    smears = [list(smear_msgs(0)), list(smear_msgs(1))]

    small = [
        pltpu.make_async_copy(src, dst, small_sem.at[n])
        for n, (src, dst) in enumerate(
            (
                (code_hbm, code_ref),
                (tgt_hbm, tgt_ref),
                (pos_hbm, pos_ref),
                (lr_hbm, lr_ref),
                (gr_hbm, gr_ref),
                (rg_hbm, rg_ref),
                (gp_hbm, gp_ref),
                (coup_hbm, coup_ref),
            )
        )
    ]
    for copy in small:
        copy.start()
    loads = []
    for y in range(ny):
        loads.append(
            pltpu.make_async_copy(
                fields_ref.at[:, :, y, :], q.at[pl.ds(0, nf), y + 3], in_sem.at[3 * y]
            )
        )
        loads.append(
            pltpu.make_async_copy(vel_ref.at[1, :, y, :], q.at[nf, y + 3], in_sem.at[3 * y + 1])
        )
        loads.append(
            pltpu.make_async_copy(vel_ref.at[0, :, y, :], ux.at[y], in_sem.at[3 * y + 2])
        )
    for copy in loads:
        copy.start()

    barrier = pltpu.get_barrier_semaphore()
    neighbours = jnp.int32(0)
    for c in DIRS:
        ok = inside(c, 1)

        @pl.when(ok)
        def _():
            pl.semaphore_signal(
                barrier,
                inc=1,
                device_id=(me_x + (c // 3 - 1), me_y + (c % 3 - 1)),
                device_id_type=pl.DeviceIdType.MESH,
            )

        neighbours = neighbours + ok.astype(jnp.int32)

    for copy in small:
        copy.wait()
    code = code_ref[0]
    target = tgt_ref[0]
    for r in range(3):
        vals[pl.ds(r, 1), :] = pos_ref[r, 0]
    vals[pl.ds(3, 1), :] = lr_ref[0]
    vals[pl.ds(4, 1), :] = gr_ref[0]
    vals[pl.ds(5, 1), :] = rg_ref[0]
    vals[pl.ds(6, 1), :] = gp_ref[0]
    vals[pl.ds(7, 1), :] = (target + 1).astype(f32)
    parts = split3_rows(vals[...])
    row16 = lax.broadcasted_iota(jnp.int32, (16, slots), 0)
    moves = jnp.where((row16 == code) & (row16 != 4) & (row16 < 9), 1.0, 0.0).astype(f32)
    chunks = slots // 128
    stacked = jnp.concatenate(
        [moves[:, 128 * k : 128 * (k + 1)] for k in range(chunks)], axis=0
    )
    upper = lax.broadcasted_iota(jnp.int32, (128, 128), 0) < lax.broadcasted_iota(
        jnp.int32, (128, 128), 1
    )
    before = dot(
        stacked.astype(jnp.bfloat16), jnp.where(upper, 1.0, 0.0).astype(jnp.bfloat16), False
    )
    offset = jnp.zeros((16, 1), f32)
    ranks = []
    for k in range(chunks):
        chunk = stacked[16 * k : 16 * (k + 1)]
        ranks.append(
            jnp.sum(chunk * (before[16 * k : 16 * (k + 1)] + offset), axis=0, keepdims=True)
        )
        offset = offset + jnp.sum(chunk, axis=1, keepdims=True)
    rank = jnp.concatenate(ranks, axis=1)
    row128 = lax.broadcasted_iota(jnp.int32, (128, slots), 0)
    pick = jnp.where(row128.astype(f32) == rank, 1.0, 0.0).astype(jnp.bfloat16)
    masked = jnp.concatenate([jnp.where(code == c, parts, 0.0) for c in DIRS], axis=0)
    boxes = dot(masked.astype(jnp.bfloat16), pick, True)
    for n in range(8):
        outbox[n] = (
            boxes[24 * n : 24 * n + 8] + boxes[24 * n + 8 : 24 * n + 16]
        ) + boxes[24 * n + 16 : 24 * n + 24]

    half = nz * ny // 128
    band = ny // half
    width = 2 * nx
    early = 5

    def columns(count, body):
        lax.fori_loop(0, count, lambda n, carry: (body(n), carry)[1], 0)

    def face_rows(buf, first, count, f, z):
        rows_q = [buf[f, first + i, z] for i in range(count + 5)]
        flux = [q[nf, first + i, z] * rows_q[i] for i in range(count + 5)]
        dq = [rows_q[i + 1] - rows_q[i] for i in range(count + 4)]
        df = [flux[i + 1] - flux[i] for i in range(count + 4)]
        for j in range(count):
            yface[f, first + j, z] = face_flux(
                dq[j : j + 5], df[j : j + 5], flux[j + 2] + flux[j + 3], topy[first + j, z]
            )

    def y_faces(buf, ranges):
        def body(n):
            z = pl.ds(pl.multiple_of((n % (nz // 8)) * 8, 8), 8)
            for first, count in ranges:
                face_rows(buf, first, count, n // (nz // 8), z)

        columns(nf * (nz // 8), body)

    def y_tops(first, count):
        for k in range(first, first + count):
            topy[k] = split_max([q[nf, k + i] for i in range(6)])

    def x_tops(blocks):
        for h in range(half):
            for b in blocks:
                topx[h, pl.ds(8 * b, 8)] = split_max(
                    [qt[nf, h, pl.ds(8 * b + 5 + i, 8)] for i in range(6)]
                )

    def x_cells(buf, f, h, blocks):
        for b in blocks:
            at, after = pl.ds(8 * b, 8), pl.ds(8 * b + 1, 8)
            here, there = buf[f, h, at], buf[f, h, after]
            flux_here, flux_there = qt[nf, h, at] * here, qt[nf, h, after] * there
            dq_s[at] = there - here
            df_s[at] = flux_there - flux_here
            pair_s[at] = flux_there + flux_here

    def x_faces(f, h, blocks):
        for b in blocks:
            dq = [dq_s[pl.ds(8 * b + 5 + i, 8)] for i in range(5)]
            df = [df_s[pl.ds(8 * b + 5 + i, 8)] for i in range(5)]
            xface[f, h, pl.ds(8 * b, 8)] = face_flux(
                dq, df, pair_s[pl.ds(8 * b + 7, 8)], topx[h, pl.ds(8 * b, 8)]
            )

    last = nx // 8

    def inner_x(buf):
        def body(n):
            f, h = n // half, n % half
            x_cells(buf, f, h, range(1, last + 1))
            x_faces(f, h, range(1, last - 1))

        columns(nf * half, body)

    def outer_x(buf):
        def body(n):
            f, h = n // half, n % half
            x_cells(buf, f, h, (0, 1, 2, last - 1, last, last + 1))
            x_faces(f, h, (0, last - 1, last))
            blocks = [
                xface[f, h, pl.ds(8 * b + 1, 8)] - xface[f, h, pl.ds(8 * b, 8)]
                for b in range(last)
            ]
            turned = jnp.concatenate(blocks, axis=0).T
            dv[f, pl.ds(pl.multiple_of(h * band, band), band)] = turned.reshape(band, nz, nx)

        columns(nf * half, body)

    def turn(value):
        return value.reshape(128, nx).T

    def pack_rims(buf, count, packed):
        for f in range(count):
            for h in range(half):
                to = pl.ds(3 * (f * half + h), 3)
                packed[0, to] = buf[f, h, pl.ds(8, 3)]
                packed[1, to] = buf[f, h, pl.ds(nx + 5, 3)]

    def unpack_rims(buf, count, got):
        for f in range(count):
            for h in range(half):
                at = pl.ds(3 * (f * half + h), 3)
                buf[f, h, pl.ds(nx + 8, 3)] = got[0, at]
                buf[f, h, pl.ds(5, 3)] = got[1, at]

    wx[pl.ds(nx, nx)] = jnp.zeros((nx, slots), jnp.bfloat16)
    wx[pl.ds(width + nx, nx)] = jnp.zeros((nx, slots), jnp.bfloat16)
    wx[pl.ds(2 * width + nx, nx)] = jnp.zeros((nx, slots), jnp.bfloat16)
    tb[...] = jnp.zeros(tb.shape, f32)

    for copy in loads:
        copy.wait()
    for h in range(half):
        for f in range(nf):
            qt[f, h, pl.ds(8, nx)] = turn(q[f, pl.ds(3 + h * band, band)])
        qt[nf, h, pl.ds(8, nx)] = turn(ux[pl.ds(h * band, band)])
    pack_rims(qt, nf + 1, pk)
    y_tops(3, ny - 5)
    y_faces(q, [(3, early)])

    pl.semaphore_wait(barrier, neighbours)
    for c, src, dst in bubble_msgs:
        send(0, c, src, dst)
    for c, src, dst in rims0:
        send(1, c, src, dst)

    x_tops(range(1, last - 1))
    inner_x(qt)
    y_faces(q, [(3 + early, ny - 5 - early)])

    for c, src, dst in bubble_msgs:
        recv(0, c, src, dst)
    stay = jnp.where(code == 4, vals[...], 0.0)
    all_vals = jnp.concatenate([stay] + [inbox[n] for n in range(8)], axis=1)
    slot = all_vals[7:8].astype(jnp.int32) - 1
    slot_hi = slot >> 7
    slot_lo = slot & 127
    total = all_vals.shape[1]
    place = jnp.where(
        lax.broadcasted_iota(jnp.int32, (128, total), 0) == slot_lo, 1.0, 0.0
    ).astype(jnp.bfloat16)
    all_parts = split3_rows(all_vals)
    spread = jnp.concatenate(
        [jnp.where(slot_hi == h, all_parts, 0.0) for h in range(chunks)], axis=0
    )
    homes = dot(spread.astype(jnp.bfloat16), place, True)
    bubbles = jnp.concatenate(
        [
            (homes[24 * h : 24 * h + 8] + homes[24 * h + 8 : 24 * h + 16])
            + homes[24 * h + 16 : 24 * h + 24]
            for h in range(chunks)
        ],
        axis=1,
    )
    occupied = jnp.where(bubbles[7:8] > 0.5, 1.0, 0.0)
    local_x = bubbles[0:1] - (me_x * nx).astype(f32)
    local_y = bubbles[1:2] - (me_y * ny).astype(f32)

    def put_weight(row, first, count):
        cell = first + lax.broadcasted_iota(jnp.int32, (count, slots), 0)
        hi, lo = split2(tent(local_x - (cell.astype(f32) + 0.5)))
        wx[pl.ds(row, count)] = hi
        wx[pl.ds(width + row, count)] = hi
        wx[pl.ds(2 * width + row, count)] = lo

    put_weight(0, 0, nx)
    put_weight(nx, nx, 16)
    put_weight(width - 16, -16, 16)
    z_dist = jnp.abs(
        bubbles[2:3] - (lax.broadcasted_iota(jnp.int32, (nz, slots), 0).astype(f32) + 0.5)
    )
    weight_z = tent(jnp.minimum(z_dist, nz - z_dist))
    for ye in range(ny + 4):
        wzy[pl.ds(ye * nz, nz)] = weight_z * tent(local_y - (ye - 1.5))

    rows = (ny + 4) * nz
    step_rows = rows // 4

    def pack_rows(rows):
        packed = jnp.zeros((nz, nx), f32)
        for y, row in rows:
            packed = jnp.where(group == y, pltpu.roll(row, (8 * y + 3) % nx, 1), packed)
        return packed

    def sampled():
        sums = []
        for n in range(slots // 256):
            at = pl.ds(256 * n, 256)
            prod = dot(samp[...], wx[:, at], False) * wzy[:, at]
            part = prod[0:8]
            for k in range(1, rows // 8):
                part = part + prod[8 * k : 8 * (k + 1)]
            sums.append(jnp.sum(part, axis=0, keepdims=True))
        return jnp.concatenate(sums, axis=1)

    def deposit(s, volume):
        for k in range(4):
            at = pl.ds(k * step_rows, step_rows)
            hi, lo = split2(wzy[at] * volume)
            part_s[at] = hi
            part_s[pl.ds(rows + k * step_rows, step_rows)] = lo
        both = dot(part_s[...], wx[pl.ds(0, width)], True)
        d = (both[:rows] + both[rows:]) + dot(
            part_s[pl.ds(0, rows)], wx[pl.ds(2 * width, width)], True
        )
        rims = []
        for r in range(ny + 4):
            dep[s, r] = d[r * nz : (r + 1) * nz, :nx]
            rims.append(d[r * nz : (r + 1) * nz, nx:])
        depx[s] = pack_rows([(y, rims[y + 2]) for y in range(ny)])
        depc[s] = pack_rows(
            [(0, rims[ny + 2]), (1, rims[ny + 3]), (ny - 2, rims[0]), (ny - 1, rims[1])]
        )
        for c, src, dst in smears[s]:
            send(2 + s, c, src, dst)

    def gather_smear(s):
        for c, src, dst in smears[s]:
            recv(2 + s, c, src, dst)
        low = lane < nx // 2
        from_right = dx_in[s, 0] + jnp.where(low, dc_in[s, 1], dc_in[s, 0])
        from_left = dx_in[s, 1] + jnp.where(low, dc_in[s, 3], dc_in[s, 2])
        merged = jnp.where(sub >= 3, from_left, from_right)
        edge = (lane < 2) | (lane >= nx - 2)
        for y in range(ny):
            total_row = dep[s, y + 2] + jnp.where(
                edge, pltpu.roll(merged, (nx - 8 * y - 3) % nx, 1), 0.0
            )
            if y < 2:
                total_row = total_row + dy_in[s, 1, y]
            if y >= ny - 2:
                total_row = total_row + dy_in[s, 0, y - (ny - 2)]
            smear[y] = total_row

    def put_sample(row, col, value):
        hi, lo = split2(value)
        count = value.shape[0]
        samp[pl.ds(row, count), pl.ds(col, nx)] = hi
        samp[pl.ds(row, count), pl.ds(width + col, nx)] = lo
        samp[pl.ds(row, count), pl.ds(2 * width + col, nx)] = hi

    def fill_sample(buf, buft, corner):
        for ye in range(ny + 4):
            put_sample(ye * nz, 0, buf[0, ye + 1])
        lanes = lax.broadcasted_iota(jnp.int32, (3, 128), 1)
        top = lanes >= 128 - 2 * nz
        final = 3 * (half - 1)
        for h in range(half):
            tb[h, pl.ds(0, 3)] = buft[0, h, pl.ds(nx + 8, 3)]
            tb[h, pl.ds(nx - 3, 3)] = buft[0, h, pl.ds(5, 3)]
        tb[half, pl.ds(0, 3)] = jnp.where(top, corner[1, pl.ds(final, 3)], corner[0, pl.ds(0, 3)])
        tb[half, pl.ds(nx - 3, 3)] = jnp.where(
            top, corner[3, pl.ds(final, 3)], corner[2, pl.ds(0, 3)]
        )
        for h in range(half):
            put_sample(2 * nz + 128 * h, nx, tb[h].T)
        turned = tb[half].T
        put_sample(0, nx, turned[128 - 2 * nz :])
        put_sample((ny + 2) * nz, nx, turned[: 2 * nz])

    rest_log = bubbles[3:4] + bubbles[5:6]
    pressure_gas = bubbles[6:7]

    def rate_of(s, w, sampled_field):
        gap = (
            pressure_gas * jnp.exp(-3.0 * (s - rest_log)) - 1.0 - 0.5 * sampled_field - 0.2 * w
        )
        return gap * jnp.exp(-2.0 * s) - 2.5 * w * w

    def volume_of(s, w):
        return occupied * four_pi * jnp.exp(3.0 * s) * w

    s_zero, w_zero = bubbles[3:4], bubbles[4:5]
    deposit(0, volume_of(s_zero, w_zero))

    for c, src, dst in rims0:
        recv(1, c, src, dst)
    unpack_rims(qt, nf + 1, pk_in)
    fill_sample(q, qt, c_in)
    s_one = s_zero + time_step * w_zero
    w_one = w_zero + time_step * rate_of(s_zero, w_zero, sampled())
    deposit(1, volume_of(s_one, w_one))

    y_tops(0, 3)
    y_tops(ny - 2, 3)
    x_tops((0, last - 1, last))
    y_faces(q, [(0, 3), (ny - 2, 3)])
    outer_x(qt)

    gather_smear(0)
    for y in range(ny):
        source = time_step * smear[y]
        for f in range(nf):
            div = dv[f, y] + (yface[f, y + 1] - yface[f, y])
            q1[f, y + 3] = (q[f, y + 3] - (time_step * flux_unit) * div) + coup_ref[f] * source
    for c, src, dst in rims1[:2]:
        send(4, c, src, dst)
    for h in range(half):
        for f in range(nf):
            qt1[f, h, pl.ds(8, nx)] = turn(q1[f, pl.ds(3 + h * band, band)])
    pack_rims(qt1, nf, pk1)
    for c, src, dst in rims1[2:]:
        send(4, c, src, dst)

    inner_x(qt1)
    y_faces(q1, [(3, ny - 5)])
    for c, src, dst in rims1:
        recv(4, c, src, dst)
    unpack_rims(qt1, nf, pk1_in)
    fill_sample(q1, qt1, c1_in)
    rate_two = rate_of(s_one, w_one, sampled())
    s_two = 0.5 * s_zero + 0.5 * (s_one + time_step * w_one)
    w_two = 0.5 * w_zero + 0.5 * (w_one + time_step * rate_two)
    bub_ref[0, 0] = s_two * occupied
    bub_ref[1, 0] = w_two * occupied
    y_faces(q1, [(0, 3), (ny - 2, 3)])
    outer_x(qt1)
    gather_smear(1)
    stores = []
    for y in range(ny):
        source = (0.5 * time_step) * smear[y]
        for f in range(nf):
            div = dv[f, y] + (yface[f, y + 1] - yface[f, y])
            stage[f, y] = (
                0.5 * (q[f, y + 3] + q1[f, y + 3]) - (0.5 * time_step * flux_unit) * div
            ) + coup_ref[f] * source
        stores.append(
            pltpu.make_async_copy(stage.at[:, y], out_ref.at[:, :, y, :], out_sem.at[y])
        )
        stores[y].start()
    for copy in stores:
        copy.wait()

    for kind, msgs in ((0, bubble_msgs), (1, rims0), (2, smears[0]), (3, smears[1]), (4, rims1)):
        for c, src, dst in msgs:
            sent(kind, c, src, dst)


def shards(n_gx, n_gy, fields, velocity, coupling, positions, log_radius, growth, rest_gap,
           gas_pressure, move_codes, targets):
    nf, nz, ny, nx = fields.shape
    slots = move_codes.shape[2]
    vmem = pl.BlockSpec(memory_space=pltpu.VMEM)
    f32 = jnp.float32
    rows = (ny + 4) * nz
    half = nz * ny // 128
    deep = nx + 24
    packed = -(-3 * half * (nf + 1) // 8) * 8
    sc = lambda *shape: pltpu.VMEM(shape, f32)
    out, bub = pl.pallas_call(
        functools.partial(kernel, n_gx, n_gy, (nf, nz, ny, nx, slots)),
        out_shape=(
            pltpu.VMEM((nf, nz, ny, nx), f32),
            pltpu.VMEM((2, 1, 1, slots), f32),
        ),
        in_specs=[pl.BlockSpec(memory_space=pltpu.HBM)] * 10,
        out_specs=(vmem, vmem),
        scratch_shapes=[
            pltpu.SMEM((nf,), f32),
            sc(3, 1, 1, slots),
            sc(1, 1, slots),
            sc(1, 1, slots),
            sc(1, 1, slots),
            sc(1, 1, slots),
            pltpu.VMEM((1, 1, slots), jnp.int32),
            pltpu.VMEM((1, 1, slots), jnp.int32),
            pltpu.SemaphoreType.DMA((8,)),
            sc(nf + 1, ny + 6, nz, nx),
            sc(nf, ny + 6, nz, nx),
            sc(ny, nz, nx),
            sc(nf + 1, half, deep, 128),
            sc(nf, half, deep, 128),
            sc(ny + 1, nz, nx),
            sc(half, nx + 8, 128),
            sc(deep, 128),
            sc(deep, 128),
            sc(deep, 128),
            sc(nf, half, nx + 16, 128),
            sc(nf, ny, nz, nx),
            sc(2, packed, 128),
            sc(2, packed, 128),
            sc(4, 8, 128),
            sc(2, packed, 128),
            sc(2, packed, 128),
            sc(4, 8, 128),
            sc(half + 1, 128, 128),
            sc(8, 8, 128),
            sc(8, 8, 128),
            sc(8, slots),
            pltpu.VMEM((rows, 6 * nx), jnp.bfloat16),
            pltpu.VMEM((6 * nx, slots), jnp.bfloat16),
            sc(rows, slots),
            pltpu.VMEM((2 * rows, slots), jnp.bfloat16),
            sc(2, ny + 4, nz, nx),
            sc(2, nz, nx),
            sc(2, nz, nx),
            sc(2, 2, 2, nz, nx),
            sc(2, 2, nz, nx),
            sc(2, 4, nz, nx),
            sc(ny, nz, nx),
            sc(nf, ny + 1, nz, nx),
            sc(ny + 4, nz, nx),
            sc(nf, ny, nz, nx),
            pltpu.SemaphoreType.DMA((3 * ny,)),
            pltpu.SemaphoreType.DMA((ny,)),
            pltpu.SemaphoreType.DMA((5, 9)),
            pltpu.SemaphoreType.DMA((5, 9)),
        ],
        compiler_params=pltpu.CompilerParams(
            collective_id=0, has_side_effects=True
        ),
    )(fields, velocity, coupling, positions, log_radius, growth, rest_gap, gas_pressure,
      move_codes, targets)
    return out, bub


def solution(mesh):
    placed = (
        P(None, None, "gy", "gx"),
        P(None, None, "gy", "gx"),
        P(),
        P(None, "gx", "gy", None),
        P("gx", "gy", None),
        P("gx", "gy", None),
        P("gx", "gy", None),
        P("gx", "gy", None),
        P("gx", "gy", None),
        P("gx", "gy", None),
    )
    return jax.shard_map(
        functools.partial(shards, mesh.shape["gx"], mesh.shape["gy"]),
        mesh=mesh,
        in_specs=placed,
        out_specs=(P(None, None, "gy", "gx"), P(None, "gx", "gy", None)),
        check_vma=False,
    )
```

```python
import functools
import math

import jax
import jax.numpy as jnp
from jax import lax
from jax.experimental import pallas as pl
from jax.experimental.pallas import tpu as pltpu
from jax.sharding import PartitionSpec as P

time_step = 0.2
four_pi = 4.0 * math.pi
smooth_eps = 3e-6
flux_unit = 1.0 / 12.0

DIRS = [c for c in range(9) if c != 4]
X_DIRS = (1, 7)
Y_DIRS = (3, 5)
DIAG = (0, 2, 6, 8)
pieces = 3


def weno_side(d1, d2, d3, d4):
    t1 = d2 - d1
    t2 = d3 - d2
    t3 = d4 - d3
    x = 0.75 * d2
    y = 0.75 * d3
    b0 = t1 * (t1 + x) + (x * d2 + smooth_eps)
    b1 = t2 * t2 + (x * d3 + smooth_eps)
    b2 = t3 * (t3 - y) + (y * d3 + smooth_eps)
    j1 = b0 / b1
    j2 = b0 / b2
    w2 = (1.5 * j2) * j2
    w1 = (3.0 * j1) * j1
    return ((t1 - t2) + w2 * (t2 - t3)) / (w2 + w1 + 0.5) - t2


def face_flux(dq, df, pair, top):
    p = [top * d for d in dq]
    r = [df[i] + p[i] for i in range(4)]
    l = [df[i + 1] - p[i + 1] for i in range(4)]
    return 6.0 * pair + (weno_side(*r) - weno_side(l[3], l[2], l[1], l[0]))


def split_max(u):
    a = [jnp.abs(v) for v in u]
    return jnp.maximum(
        jnp.maximum(jnp.maximum(a[0], a[1]), jnp.maximum(a[2], a[3])), jnp.maximum(a[4], a[5])
    )


def split2(v):
    hi = v.astype(jnp.bfloat16)
    lo = (v - hi.astype(jnp.float32)).astype(jnp.bfloat16)
    return hi, lo


def split3_rows(v):
    hi = v.astype(jnp.bfloat16).astype(jnp.float32)
    rest = v - hi
    mid = rest.astype(jnp.bfloat16).astype(jnp.float32)
    return jnp.concatenate([hi, mid, rest - mid], axis=0)


def tent(d):
    return jnp.maximum(0.0, 0.5 - jnp.abs(0.25 * d))


def dot(a, b, trans):
    dims = (((1,), (1,)), ((), ())) if trans else (((1,), (0,)), ((), ()))
    return lax.dot_general(a, b, dims, preferred_element_type=jnp.float32)


def kernel(
    n_gx,
    n_gy,
    dims,
    fields_ref,
    vel_ref,
    coup_hbm,
    pos_hbm,
    lr_hbm,
    gr_hbm,
    rg_hbm,
    gp_hbm,
    code_hbm,
    tgt_hbm,
    out_ref,
    bub_ref,
    coup_ref,
    pos_ref,
    lr_ref,
    gr_ref,
    rg_ref,
    gp_ref,
    code_ref,
    tgt_ref,
    small_sem,
    q,
    q1,
    ux,
    qt,
    qt1,
    topy,
    topx,
    dq_s,
    df_s,
    pair_s,
    xface,
    dv,
    pk,
    pk_in,
    c_in,
    pk1,
    pk1_in,
    c1_in,
    tb,
    outbox,
    inbox,
    vals,
    samp,
    wx,
    wzy,
    part_s,
    dep,
    depx,
    depc,
    dy_in,
    dx_in,
    dc_in,
    yface,
    in_sem,
    send_sem,
    recv_sem,
):
    nf, nz, ny, nx, slots = dims
    f32 = jnp.float32
    me_x = lax.axis_index("gx")
    me_y = lax.axis_index("gy")
    lane = lax.broadcasted_iota(jnp.int32, (nz, nx), 1)
    group = lane // 8
    sub = lane % 8

    def inside(c, sign):
        a, b = sign * (c // 3 - 1), sign * (c % 3 - 1)
        ok = None
        for pos, step, count in ((me_x, a, n_gx), (me_y, b, n_gy)):
            cond = None
            if step == 1:
                cond = pos < count - 1
            elif step == -1:
                cond = pos > 0
            if cond is not None:
                ok = cond if ok is None else jnp.logical_and(ok, cond)
        return ok

    def desc(kind, c, src, dst):
        return pltpu.make_async_remote_copy(
            src_ref=src,
            dst_ref=dst,
            send_sem=send_sem.at[kind, c],
            recv_sem=recv_sem.at[kind, c],
            device_id=(me_x + (c // 3 - 1), me_y + (c % 3 - 1)),
            device_id_type=pl.DeviceIdType.MESH,
        )

    def send(kind, c, src, dst):
        @pl.when(inside(c, 1))
        def _():
            desc(kind, c, src, dst).start()

    def sent(kind, c, src, dst):
        @pl.when(inside(c, 1))
        def _():
            desc(kind, c, src, dst).wait_send()

    def recv(kind, c, src, dst):
        @pl.when(inside(c, -1))
        def _():
            desc(kind, c, src, dst).wait_recv()

        @pl.when(jnp.logical_not(inside(c, -1)))
        def _():
            dst[...] = jnp.zeros(dst.shape, f32)

    def y_msgs(buf, first, count):
        f = pl.ds(first, count)
        yield 3, buf.at[f, pl.ds(3, 3)], buf.at[f, pl.ds(ny + 3, 3)]
        yield 5, buf.at[f, pl.ds(ny, 3)], buf.at[f, pl.ds(0, 3)]

    def rim_msgs(packed, packed_in, corner_in):
        for n, c in enumerate(X_DIRS):
            yield c, packed.at[n], packed_in.at[n]
        for n, c in enumerate(DIAG):
            yield c, packed.at[n // 2, pl.ds(0, 8)], corner_in.at[n]

    def smear_msgs(s):
        yield 3, dep.at[s, pl.ds(0, 2)], dy_in.at[s, 0]
        yield 5, dep.at[s, pl.ds(ny + 2, 2)], dy_in.at[s, 1]
        for n, c in enumerate(X_DIRS):
            yield c, depx.at[s], dx_in.at[s, n]
        for n, c in enumerate(DIAG):
            yield c, depc.at[s], dc_in.at[s, n]

    bubble_msgs = [(c, outbox.at[n], inbox.at[n]) for n, c in enumerate(DIRS)]
    rims0 = list(rim_msgs(pk, pk_in, c_in))
    rims1 = list(rim_msgs(pk1, pk1_in, c1_in))
    group_of = nf // pieces
    y_rims0 = [list(y_msgs(q, p * group_of, group_of)) for p in range(pieces)]
    y_rims1 = [list(y_msgs(q1, p * group_of, group_of)) for p in range(pieces)]
    y_speed = list(y_msgs(q, nf, 1))
    smears = [list(smear_msgs(0)), list(smear_msgs(1))]

    small = [
        pltpu.make_async_copy(src, dst, small_sem.at[n])
        for n, (src, dst) in enumerate(
            (
                (code_hbm, code_ref),
                (tgt_hbm, tgt_ref),
                (pos_hbm, pos_ref),
                (lr_hbm, lr_ref),
                (gr_hbm, gr_ref),
                (rg_hbm, rg_ref),
                (gp_hbm, gp_ref),
                (coup_hbm, coup_ref),
            )
        )
    ]
    for copy in small:
        copy.start()
    loads = []
    for y in range(ny):
        loads.append(
            pltpu.make_async_copy(
                fields_ref.at[:, :, y, :], q.at[pl.ds(0, nf), y + 3], in_sem.at[3 * y]
            )
        )
        loads.append(
            pltpu.make_async_copy(vel_ref.at[1, :, y, :], q.at[nf, y + 3], in_sem.at[3 * y + 1])
        )
        loads.append(
            pltpu.make_async_copy(vel_ref.at[0, :, y, :], ux.at[y], in_sem.at[3 * y + 2])
        )
    for copy in loads:
        copy.start()

    barrier = pltpu.get_barrier_semaphore()
    neighbours = jnp.int32(0)
    for c in DIRS:
        ok = inside(c, 1)

        @pl.when(ok)
        def _():
            pl.semaphore_signal(
                barrier,
                inc=1,
                device_id=(me_x + (c // 3 - 1), me_y + (c % 3 - 1)),
                device_id_type=pl.DeviceIdType.MESH,
            )

        neighbours = neighbours + ok.astype(jnp.int32)

    for copy in small:
        copy.wait()
    code = code_ref[0]
    target = tgt_ref[0]
    for r in range(3):
        vals[pl.ds(r, 1), :] = pos_ref[r, 0]
    vals[pl.ds(3, 1), :] = lr_ref[0]
    vals[pl.ds(4, 1), :] = gr_ref[0]
    vals[pl.ds(5, 1), :] = rg_ref[0]
    vals[pl.ds(6, 1), :] = gp_ref[0]
    vals[pl.ds(7, 1), :] = (target + 1).astype(f32)
    parts = split3_rows(vals[...])
    row16 = lax.broadcasted_iota(jnp.int32, (16, slots), 0)
    moves = jnp.where((row16 == code) & (row16 != 4) & (row16 < 9), 1.0, 0.0).astype(f32)
    chunks = slots // 128
    stacked = jnp.concatenate(
        [moves[:, 128 * k : 128 * (k + 1)] for k in range(chunks)], axis=0
    )
    upper = lax.broadcasted_iota(jnp.int32, (128, 128), 0) < lax.broadcasted_iota(
        jnp.int32, (128, 128), 1
    )
    before = dot(
        stacked.astype(jnp.bfloat16), jnp.where(upper, 1.0, 0.0).astype(jnp.bfloat16), False
    )
    offset = jnp.zeros((16, 1), f32)
    ranks = []
    for k in range(chunks):
        chunk = stacked[16 * k : 16 * (k + 1)]
        ranks.append(
            jnp.sum(chunk * (before[16 * k : 16 * (k + 1)] + offset), axis=0, keepdims=True)
        )
        offset = offset + jnp.sum(chunk, axis=1, keepdims=True)
    rank = jnp.concatenate(ranks, axis=1)
    row128 = lax.broadcasted_iota(jnp.int32, (128, slots), 0)
    pick = jnp.where(row128.astype(f32) == rank, 1.0, 0.0).astype(jnp.bfloat16)
    masked = jnp.concatenate([jnp.where(code == c, parts, 0.0) for c in DIRS], axis=0)
    boxes = dot(masked.astype(jnp.bfloat16), pick, True)
    for n in range(8):
        outbox[n] = (
            boxes[24 * n : 24 * n + 8] + boxes[24 * n + 8 : 24 * n + 16]
        ) + boxes[24 * n + 16 : 24 * n + 24]

    half = nz * ny // 128
    band = ny // half
    width = 2 * nx
    lanes_at_once = 3
    tiles = slots // 256

    def face_rows(buf, first, count, f, z):
        rows_q = [buf[f, first + i, z] for i in range(count + 5)]
        flux = [q[nf, first + i, z] * rows_q[i] for i in range(count + 5)]
        dq = [rows_q[i + 1] - rows_q[i] for i in range(count + 4)]
        df = [flux[i + 1] - flux[i] for i in range(count + 4)]
        for j in range(count):
            yface[f, first + j, z] = face_flux(
                dq[j : j + 5], df[j : j + 5], flux[j + 2] + flux[j + 3], topy[first + j, z]
            )

    def y_tops(first, count):
        for k in range(first, first + count):
            topy[k] = split_max([q[nf, k + i] for i in range(6)])

    def x_tops(blocks):
        for h in range(half):
            for b in blocks:
                topx[h, pl.ds(8 * b, 8)] = split_max(
                    [qt[nf, h, pl.ds(8 * b + 5 + i, 8)] for i in range(6)]
                )

    def x_cells(buf, f, h, blocks, dq_s, df_s, pair_s):
        for b in blocks:
            at, after = pl.ds(8 * b, 8), pl.ds(8 * b + 1, 8)
            here, there = buf[f, h, at], buf[f, h, after]
            flux_here, flux_there = qt[nf, h, at] * here, qt[nf, h, after] * there
            dq_s[at] = there - here
            df_s[at] = flux_there - flux_here
            pair_s[at] = flux_there + flux_here

    def x_faces(f, h, blocks, dq_s, df_s, pair_s):
        for b in blocks:
            dq = [dq_s[pl.ds(8 * b + 5 + i, 8)] for i in range(5)]
            df = [df_s[pl.ds(8 * b + 5 + i, 8)] for i in range(5)]
            xface[f, h, pl.ds(8 * b, 8)] = face_flux(
                dq, df, pair_s[pl.ds(8 * b + 7, 8)], topx[h, pl.ds(8 * b, 8)]
            )

    last = nx // 8

    def halves(h):
        return pl.ds(pl.multiple_of(h * 8, 8), 8)

    def inner_columns(buf, buft, first, stop):
        def body(k, carry):
            for j in range(lanes_at_once):
                n = k * lanes_at_once + j
                f, h = n // half, n % half
                work = (dq_s.at[j], df_s.at[j], pair_s.at[j])
                x_cells(buft, f, h, range(1, last + 1), *work)
                x_faces(f, h, range(1, last - 1), *work)
                face_rows(buf, 3, ny - 5, f, halves(h))
            return carry

        lax.fori_loop(first, stop, body, 0)

    def outer_column(buf, buft, f, h, slot):
        work = (dq_s.at[slot], df_s.at[slot], pair_s.at[slot])
        x_cells(buft, f, h, (0, 1, 2, last - 1, last, last + 1), *work)
        x_faces(f, h, (0, last - 1, last), *work)
        blocks = [
            xface[f, h, pl.ds(8 * b + 1, 8)] - xface[f, h, pl.ds(8 * b, 8)] for b in range(last)
        ]
        turned = jnp.concatenate(blocks, axis=0).T
        dv[f, pl.ds(h * band, band)] = turned.reshape(band, nz, nx)
        face_rows(buf, 0, 3, f, halves(h))
        face_rows(buf, ny - 2, 3, f, halves(h))

    def outer_columns(buf, buft, y_rims, kind):
        sums = []
        for p in range(pieces):
            if p:
                for c, src, dst in y_rims[p]:
                    recv(kind + p, c, src, dst)
            for n in range(p * group_of * half, (p + 1) * group_of * half):
                outer_column(buf, buft, n // half, n % half, n % 4)
            for n in range(p * tiles // pieces, (p + 1) * tiles // pieces):
                sums.append(sample_tile(n))
        return jnp.concatenate(sums, axis=1)

    def turn(value):
        return value.reshape(128, nx).T

    def pack_rims(buf, count, packed):
        for f in range(count):
            for h in range(half):
                to = pl.ds(3 * (f * half + h), 3)
                packed[0, to] = buf[f, h, pl.ds(8, 3)]
                packed[1, to] = buf[f, h, pl.ds(nx + 5, 3)]

    def unpack_rims(buf, count, got):
        for f in range(count):
            for h in range(half):
                at = pl.ds(3 * (f * half + h), 3)
                buf[f, h, pl.ds(nx + 8, 3)] = got[0, at]
                buf[f, h, pl.ds(5, 3)] = got[1, at]

    wx[pl.ds(nx, nx)] = jnp.zeros((nx, slots), jnp.bfloat16)
    wx[pl.ds(width + nx, nx)] = jnp.zeros((nx, slots), jnp.bfloat16)
    wx[pl.ds(2 * width + nx, nx)] = jnp.zeros((nx, slots), jnp.bfloat16)
    tb[...] = jnp.zeros(tb.shape, f32)

    for copy in loads:
        copy.wait()
    for h in range(half):
        for f in range(nf):
            qt[f, h, pl.ds(8, nx)] = turn(q[f, pl.ds(3 + h * band, band)])
        qt[nf, h, pl.ds(8, nx)] = turn(ux[pl.ds(h * band, band)])
    pack_rims(qt, nf + 1, pk)
    y_tops(3, ny - 5)
    x_tops(range(1, last - 1))
    inner_columns(q, qt, 0, 1)

    pl.semaphore_wait(barrier, neighbours)
    for c, src, dst in bubble_msgs:
        send(0, c, src, dst)
    for c, src, dst in y_speed:
        send(8, c, src, dst)
    for c, src, dst in y_rims0[0]:
        send(5, c, src, dst)
    for c, src, dst in rims0:
        send(1, c, src, dst)
    for p in range(1, pieces):
        for c, src, dst in y_rims0[p]:
            send(5 + p, c, src, dst)

    inner_columns(q, qt, 1, nf * half // lanes_at_once)

    for c, src, dst in bubble_msgs:
        recv(0, c, src, dst)
    stay = jnp.where(code == 4, vals[...], 0.0)
    all_vals = jnp.concatenate([stay] + [inbox[n] for n in range(8)], axis=1)
    slot = all_vals[7:8].astype(jnp.int32) - 1
    slot_hi = slot >> 7
    slot_lo = slot & 127
    total = all_vals.shape[1]
    place = jnp.where(
        lax.broadcasted_iota(jnp.int32, (128, total), 0) == slot_lo, 1.0, 0.0
    ).astype(jnp.bfloat16)
    all_parts = split3_rows(all_vals)
    spread = jnp.concatenate(
        [jnp.where(slot_hi == h, all_parts, 0.0) for h in range(chunks)], axis=0
    )
    homes = dot(spread.astype(jnp.bfloat16), place, True)
    bubbles = jnp.concatenate(
        [
            (homes[24 * h : 24 * h + 8] + homes[24 * h + 8 : 24 * h + 16])
            + homes[24 * h + 16 : 24 * h + 24]
            for h in range(chunks)
        ],
        axis=1,
    )
    occupied = jnp.where(bubbles[7:8] > 0.5, 1.0, 0.0)
    local_x = bubbles[0:1] - (me_x * nx).astype(f32)
    local_y = bubbles[1:2] - (me_y * ny).astype(f32)

    def put_weight(row, first, count):
        cell = first + lax.broadcasted_iota(jnp.int32, (count, slots), 0)
        hi, lo = split2(tent(local_x - (cell.astype(f32) + 0.5)))
        wx[pl.ds(row, count)] = hi
        wx[pl.ds(width + row, count)] = hi
        wx[pl.ds(2 * width + row, count)] = lo

    put_weight(0, 0, nx)
    put_weight(nx, nx, 16)
    put_weight(width - 16, -16, 16)
    z_dist = jnp.abs(
        bubbles[2:3] - (lax.broadcasted_iota(jnp.int32, (nz, slots), 0).astype(f32) + 0.5)
    )
    weight_z = tent(jnp.minimum(z_dist, nz - z_dist))
    for ye in range(ny + 4):
        wzy[pl.ds(ye * nz, nz)] = weight_z * tent(local_y - (ye - 1.5))

    rows = (ny + 4) * nz
    step_rows = rows // 4

    def pack_rows(rows):
        packed = jnp.zeros((nz, nx), f32)
        for y, row in rows:
            packed = jnp.where(group == y, pltpu.roll(row, (8 * y + 3) % nx, 1), packed)
        return packed

    def sample_tile(n):
        at = pl.ds(256 * n, 256)
        prod = dot(samp[...], wx[:, at], False) * wzy[:, at]
        part = prod[0:8]
        for k in range(1, rows // 8):
            part = part + prod[8 * k : 8 * (k + 1)]
        return jnp.sum(part, axis=0, keepdims=True)

    def deposit(s, volume):
        for k in range(4):
            at = pl.ds(k * step_rows, step_rows)
            hi, lo = split2(wzy[at] * volume)
            part_s[at] = hi
            part_s[pl.ds(rows + k * step_rows, step_rows)] = lo
        both = dot(part_s[...], wx[pl.ds(0, width)], True)
        d = (both[:rows] + both[rows:]) + dot(
            part_s[pl.ds(0, rows)], wx[pl.ds(2 * width, width)], True
        )
        rims = []
        for r in range(ny + 4):
            dep[s, r] = d[r * nz : (r + 1) * nz, :nx]
            rims.append(d[r * nz : (r + 1) * nz, nx:])
        depx[s] = pack_rows([(y, rims[y + 2]) for y in range(ny)])
        depc[s] = pack_rows(
            [(0, rims[ny + 2]), (1, rims[ny + 3]), (ny - 2, rims[0]), (ny - 1, rims[1])]
        )
        for c, src, dst in smears[s]:
            send(2 + s, c, src, dst)

    def gather_smear(s):
        for c, src, dst in smears[s]:
            recv(2 + s, c, src, dst)
        low = lane < nx // 2
        from_right = dx_in[s, 0] + jnp.where(low, dc_in[s, 1], dc_in[s, 0])
        from_left = dx_in[s, 1] + jnp.where(low, dc_in[s, 3], dc_in[s, 2])
        return jnp.where(sub >= 3, from_left, from_right)

    def smear_row(s, merged, y):
        edge = (lane < 2) | (lane >= nx - 2)
        total_row = dep[s, y + 2] + jnp.where(
            edge, pltpu.roll(merged, (nx - 8 * y - 3) % nx, 1), 0.0
        )
        if y < 2:
            total_row = total_row + dy_in[s, 1, y]
        if y >= ny - 2:
            total_row = total_row + dy_in[s, 0, y - (ny - 2)]
        return total_row

    def put_sample(row, col, value):
        hi, lo = split2(value)
        count = value.shape[0]
        samp[pl.ds(row, count), pl.ds(col, nx)] = hi
        samp[pl.ds(row, count), pl.ds(width + col, nx)] = lo
        samp[pl.ds(row, count), pl.ds(2 * width + col, nx)] = hi

    def fill_sample(buf, buft, corner):
        for ye in range(ny + 4):
            put_sample(ye * nz, 0, buf[0, ye + 1])
        lanes = lax.broadcasted_iota(jnp.int32, (3, 128), 1)
        top = lanes >= 128 - 2 * nz
        final = 3 * (half - 1)
        for h in range(half):
            tb[h, pl.ds(0, 3)] = buft[0, h, pl.ds(nx + 8, 3)]
            tb[h, pl.ds(nx - 3, 3)] = buft[0, h, pl.ds(5, 3)]
        tb[half, pl.ds(0, 3)] = jnp.where(top, corner[1, pl.ds(final, 3)], corner[0, pl.ds(0, 3)])
        tb[half, pl.ds(nx - 3, 3)] = jnp.where(
            top, corner[3, pl.ds(final, 3)], corner[2, pl.ds(0, 3)]
        )
        for h in range(half):
            put_sample(2 * nz + 128 * h, nx, tb[h].T)
        turned = tb[half].T
        put_sample(0, nx, turned[128 - 2 * nz :])
        put_sample((ny + 2) * nz, nx, turned[: 2 * nz])

    rest_log = bubbles[3:4] + bubbles[5:6]
    pressure_gas = bubbles[6:7]

    def rate_of(s, w, sampled_field):
        gap = (
            pressure_gas * jnp.exp(-3.0 * (s - rest_log)) - 1.0 - 0.5 * sampled_field - 0.2 * w
        )
        return gap * jnp.exp(-2.0 * s) - 2.5 * w * w

    def volume_of(s, w):
        return occupied * four_pi * jnp.exp(3.0 * s) * w

    s_zero, w_zero = bubbles[3:4], bubbles[4:5]
    deposit(0, volume_of(s_zero, w_zero))

    for c, src, dst in y_speed:
        recv(8, c, src, dst)
    for c, src, dst in rims0:
        recv(1, c, src, dst)
    for c, src, dst in y_rims0[0]:
        recv(5, c, src, dst)
    unpack_rims(qt, nf + 1, pk_in)
    fill_sample(q, qt, c_in)
    y_tops(0, 3)
    y_tops(ny - 2, 3)
    x_tops((0, last - 1, last))
    sampled = outer_columns(q, qt, y_rims0, 5)
    s_one = s_zero + time_step * w_zero
    w_one = w_zero + time_step * rate_of(s_zero, w_zero, sampled)
    deposit(1, volume_of(s_one, w_one))

    merged = gather_smear(0)

    def first_section(y):
        source = time_step * smear_row(0, merged, y)
        for f in range(nf):
            div = dv[f, y] + (yface[f, y + 1] - yface[f, y])
            q1[f, y + 3] = (q[f, y + 3] - (time_step * flux_unit) * div) + coup_ref[f] * source

    outermost = [0, 1, 2, ny - 3, ny - 2, ny - 1]
    for y in outermost:
        first_section(y)
    for p in range(pieces):
        for c, src, dst in y_rims1[p]:
            send(9 + p, c, src, dst)
    for y in range(3, ny - 3):
        first_section(y)
    for h in range(half):
        for f in range(nf):
            qt1[f, h, pl.ds(8, nx)] = turn(q1[f, pl.ds(3 + h * band, band)])
    pack_rims(qt1, nf, pk1)
    for c, src, dst in rims1:
        send(4, c, src, dst)

    inner_columns(q1, qt1, 0, nf * half // lanes_at_once)
    for c, src, dst in rims1:
        recv(4, c, src, dst)
    for c, src, dst in y_rims1[0]:
        recv(9, c, src, dst)
    unpack_rims(qt1, nf, pk1_in)
    fill_sample(q1, qt1, c1_in)
    rate_two = rate_of(s_one, w_one, outer_columns(q1, qt1, y_rims1, 9))
    s_two = 0.5 * s_zero + 0.5 * (s_one + time_step * w_one)
    w_two = 0.5 * w_zero + 0.5 * (w_one + time_step * rate_two)
    bub_ref[0, 0] = s_two * occupied
    bub_ref[1, 0] = w_two * occupied
    merged1 = gather_smear(1)
    for y in range(ny):
        source = (0.5 * time_step) * smear_row(1, merged1, y)
        for f in range(nf):
            div = dv[f, y] + (yface[f, y + 1] - yface[f, y])
            out_ref[f, y] = (
                0.5 * (q[f, y + 3] + q1[f, y + 3]) - (0.5 * time_step * flux_unit) * div
            ) + coup_ref[f] * source

    for kind, msgs in ((0, bubble_msgs), (1, rims0), (2, smears[0]), (3, smears[1]), (4, rims1),
                       *((5 + p, y_rims0[p]) for p in range(pieces)), (8, y_speed),
                       *((9 + p, y_rims1[p]) for p in range(pieces))):
        for c, src, dst in msgs:
            sent(kind, c, src, dst)


def write_out(fields_ref, bubbles_ref, out_ref, bub_ref, sem):
    ny = fields_ref.shape[1]
    copies = [pltpu.make_async_copy(bubbles_ref, bub_ref, sem.at[ny])]
    for y in range(ny):
        copies.append(pltpu.make_async_copy(fields_ref.at[:, y], out_ref.at[:, :, y, :], sem.at[y]))
    for copy in copies:
        copy.start()
    for copy in copies:
        copy.wait()


def shards(n_gx, n_gy, fields, velocity, coupling, positions, log_radius, growth, rest_gap,
           gas_pressure, move_codes, targets):
    nf, nz, ny, nx = fields.shape
    slots = move_codes.shape[2]
    vmem = pl.BlockSpec(memory_space=pltpu.VMEM)
    f32 = jnp.float32
    rows = (ny + 4) * nz
    half = nz * ny // 128
    deep = nx + 24
    packed = -(-3 * half * (nf + 1) // 8) * 8
    sc = lambda *shape: pltpu.VMEM(shape, f32)
    out, bub = pl.pallas_call(
        functools.partial(kernel, n_gx, n_gy, (nf, nz, ny, nx, slots)),
        out_shape=(
            pltpu.VMEM((nf, ny, nz, nx), f32),
            pltpu.VMEM((2, 1, 1, slots), f32),
        ),
        in_specs=[pl.BlockSpec(memory_space=pltpu.HBM)] * 10,
        out_specs=(vmem, vmem),
        scratch_shapes=[
            pltpu.SMEM((nf,), f32),
            sc(3, 1, 1, slots),
            sc(1, 1, slots),
            sc(1, 1, slots),
            sc(1, 1, slots),
            sc(1, 1, slots),
            pltpu.VMEM((1, 1, slots), jnp.int32),
            pltpu.VMEM((1, 1, slots), jnp.int32),
            pltpu.SemaphoreType.DMA((8,)),
            sc(nf + 1, ny + 6, nz, nx),
            sc(nf, ny + 6, nz, nx),
            sc(ny, nz, nx),
            sc(nf + 1, half, deep, 128),
            sc(nf, half, deep, 128),
            sc(ny + 1, nz, nx),
            sc(half, nx + 8, 128),
            sc(4, deep, 128),
            sc(4, deep, 128),
            sc(4, deep, 128),
            sc(nf, half, nx + 16, 128),
            sc(nf, ny, nz, nx),
            sc(2, packed, 128),
            sc(2, packed, 128),
            sc(4, 8, 128),
            sc(2, packed, 128),
            sc(2, packed, 128),
            sc(4, 8, 128),
            sc(half + 1, 128, 128),
            sc(8, 8, 128),
            sc(8, 8, 128),
            sc(8, slots),
            pltpu.VMEM((rows, 6 * nx), jnp.bfloat16),
            pltpu.VMEM((6 * nx, slots), jnp.bfloat16),
            sc(rows, slots),
            pltpu.VMEM((2 * rows, slots), jnp.bfloat16),
            sc(2, ny + 4, nz, nx),
            sc(2, nz, nx),
            sc(2, nz, nx),
            sc(2, 2, 2, nz, nx),
            sc(2, 2, nz, nx),
            sc(2, 4, nz, nx),
            sc(nf, ny + 1, nz, nx),
            pltpu.SemaphoreType.DMA((3 * ny,)),
            pltpu.SemaphoreType.DMA((12, 9)),
            pltpu.SemaphoreType.DMA((12, 9)),
        ],
        compiler_params=pltpu.CompilerParams(
            collective_id=0, has_side_effects=True
        ),
    )(fields, velocity, coupling, positions, log_radius, growth, rest_gap, gas_pressure,
      move_codes, targets)
    here = functools.partial(pltpu.with_memory_space_constraint, memory_space=pltpu.VMEM)
    return pl.pallas_call(
        write_out,
        out_shape=(
            jax.ShapeDtypeStruct((nf, nz, ny, nx), f32),
            jax.ShapeDtypeStruct((2, 1, 1, slots), f32),
        ),
        in_specs=[vmem, vmem],
        out_specs=(pl.BlockSpec(memory_space=pl.ANY), pl.BlockSpec(memory_space=pl.ANY)),
        scratch_shapes=[pltpu.SemaphoreType.DMA((ny + 1,))],
    )(here(out), here(bub))


def solution(mesh):
    placed = (
        P(None, None, "gy", "gx"),
        P(None, None, "gy", "gx"),
        P(),
        P(None, "gx", "gy", None),
        P("gx", "gy", None),
        P("gx", "gy", None),
        P("gx", "gy", None),
        P("gx", "gy", None),
        P("gx", "gy", None),
        P("gx", "gy", None),
    )
    return jax.shard_map(
        functools.partial(shards, mesh.shape["gx"], mesh.shape["gy"]),
        mesh=mesh,
        in_specs=placed,
        out_specs=(P(None, None, "gy", "gx"), P(None, "gx", "gy", None)),
        check_vma=False,
    )
```

```python
import functools
import math

import jax
import jax.numpy as jnp
from jax import lax
from jax.experimental import pallas as pl
from jax.experimental.pallas import tpu as pltpu
from jax.sharding import PartitionSpec as P

time_step = 0.2
four_pi = 4.0 * math.pi
smooth_eps = 3e-6
flux_unit = 1.0 / 12.0

DIRS = [c for c in range(9) if c != 4]
X_DIRS = (1, 7)
Y_DIRS = (3, 5)
DIAG = (0, 2, 6, 8)
pieces = 3


def weno_side(d1, d2, d3, d4):
    t1 = d2 - d1
    t2 = d3 - d2
    t3 = d4 - d3
    x = 0.75 * d2
    y = 0.75 * d3
    near = x * d2 + smooth_eps
    b0 = t1 * (t1 + x) + near
    b1 = t2 * (t2 + x) + near
    b2 = t3 * (t3 - y) + (y * d3 + smooth_eps)
    j1 = b0 / b1
    j2 = b0 / b2
    w2 = (1.5 * j2) * j2
    w1 = (3.0 * j1) * j1
    return ((t1 - t2) + w2 * (t2 - t3)) / (w2 + w1 + 0.5) - t2


def face_flux(dq, df, pair, top):
    p = [top * d for d in dq]
    r = [df[i] + p[i] for i in range(4)]
    l = [df[i + 1] - p[i + 1] for i in range(4)]
    return 6.0 * pair + (weno_side(*r) - weno_side(l[3], l[2], l[1], l[0]))


def split_max(u):
    a = [jnp.abs(v) for v in u]
    return jnp.maximum(
        jnp.maximum(jnp.maximum(a[0], a[1]), jnp.maximum(a[2], a[3])), jnp.maximum(a[4], a[5])
    )


def split2(v):
    hi = v.astype(jnp.bfloat16)
    lo = (v - hi.astype(jnp.float32)).astype(jnp.bfloat16)
    return hi, lo


def split3_rows(v):
    hi = v.astype(jnp.bfloat16).astype(jnp.float32)
    rest = v - hi
    mid = rest.astype(jnp.bfloat16).astype(jnp.float32)
    return jnp.concatenate([hi, mid, rest - mid], axis=0)


def tent(d):
    return jnp.maximum(0.0, 0.5 - jnp.abs(0.25 * d))


def dot(a, b, trans):
    dims = (((1,), (1,)), ((), ())) if trans else (((1,), (0,)), ((), ()))
    return lax.dot_general(a, b, dims, preferred_element_type=jnp.float32)


def kernel(
    n_gx,
    n_gy,
    dims,
    fields_ref,
    vel_ref,
    coup_hbm,
    pos_hbm,
    lr_hbm,
    gr_hbm,
    rg_hbm,
    gp_hbm,
    code_hbm,
    tgt_hbm,
    out_ref,
    bub_ref,
    coup_ref,
    pos_ref,
    lr_ref,
    gr_ref,
    rg_ref,
    gp_ref,
    code_ref,
    tgt_ref,
    small_sem,
    q,
    q1,
    ux,
    qt,
    qt1,
    topy,
    topx,
    dq_s,
    df_s,
    pair_s,
    xface,
    dv,
    pk,
    pk_in,
    c_in,
    pk1,
    pk1_in,
    c1_in,
    tb,
    outbox,
    inbox,
    vals,
    home_s,
    samp,
    wx,
    wzy,
    part_s,
    dep,
    depx,
    depc,
    dy_in,
    dx_in,
    dc_in,
    yface,
    in_sem,
    send_sem,
    recv_sem,
):
    nf, nz, ny, nx, slots = dims
    f32 = jnp.float32
    me_x = lax.axis_index("gx")
    me_y = lax.axis_index("gy")
    lane = lax.broadcasted_iota(jnp.int32, (nz, nx), 1)
    group = lane // 8
    sub = lane % 8

    def inside(c, sign):
        a, b = sign * (c // 3 - 1), sign * (c % 3 - 1)
        ok = None
        for pos, step, count in ((me_x, a, n_gx), (me_y, b, n_gy)):
            cond = None
            if step == 1:
                cond = pos < count - 1
            elif step == -1:
                cond = pos > 0
            if cond is not None:
                ok = cond if ok is None else jnp.logical_and(ok, cond)
        return ok

    def desc(kind, c, src, dst):
        return pltpu.make_async_remote_copy(
            src_ref=src,
            dst_ref=dst,
            send_sem=send_sem.at[kind, c],
            recv_sem=recv_sem.at[kind, c],
            device_id=(me_x + (c // 3 - 1), me_y + (c % 3 - 1)),
            device_id_type=pl.DeviceIdType.MESH,
        )

    def send(kind, c, src, dst):
        @pl.when(inside(c, 1))
        def _():
            desc(kind, c, src, dst).start()

    def sent(kind, c, src, dst):
        @pl.when(inside(c, 1))
        def _():
            desc(kind, c, src, dst).wait_send()

    def recv(kind, c, src, dst):
        @pl.when(inside(c, -1))
        def _():
            desc(kind, c, src, dst).wait_recv()

        @pl.when(jnp.logical_not(inside(c, -1)))
        def _():
            dst[...] = jnp.zeros(dst.shape, f32)

    def y_msgs(buf, first, count):
        f = pl.ds(first, count)
        yield 3, buf.at[f, pl.ds(3, 3)], buf.at[f, pl.ds(ny + 3, 3)]
        yield 5, buf.at[f, pl.ds(ny, 3)], buf.at[f, pl.ds(0, 3)]

    def rim_msgs(packed, packed_in, corner_in):
        for n, c in enumerate(X_DIRS):
            yield c, packed.at[n], packed_in.at[n]
        for n, c in enumerate(DIAG):
            yield c, packed.at[n // 2, pl.ds(0, 8)], corner_in.at[n]

    def smear_msgs(s):
        yield 3, dep.at[s, pl.ds(0, 2)], dy_in.at[s, 0]
        yield 5, dep.at[s, pl.ds(ny + 2, 2)], dy_in.at[s, 1]
        for n, c in enumerate(X_DIRS):
            yield c, depx.at[s], dx_in.at[s, n]
        for n, c in enumerate(DIAG):
            yield c, depc.at[s], dc_in.at[s, n]

    bubble_msgs = [(c, outbox.at[n], inbox.at[n]) for n, c in enumerate(DIRS)]
    rims0 = list(rim_msgs(pk, pk_in, c_in))
    rims1 = list(rim_msgs(pk1, pk1_in, c1_in))
    group_of = nf // pieces
    y_rims0 = [list(y_msgs(q, p * group_of, group_of)) for p in range(pieces)]
    y_rims1 = [list(y_msgs(q1, p * group_of, group_of)) for p in range(pieces)]
    y_speed = list(y_msgs(q, nf, 1))
    smears = [list(smear_msgs(0)), list(smear_msgs(1))]

    barrier = pltpu.get_barrier_semaphore()
    neighbours = jnp.int32(0)
    for c in DIRS:
        ok = inside(c, 1)

        @pl.when(ok)
        def _():
            pl.semaphore_signal(
                barrier,
                inc=1,
                device_id=(me_x + (c // 3 - 1), me_y + (c % 3 - 1)),
                device_id_type=pl.DeviceIdType.MESH,
            )

        neighbours = neighbours + ok.astype(jnp.int32)

    small = [
        pltpu.make_async_copy(src, dst, small_sem.at[n])
        for n, (src, dst) in enumerate(
            (
                (code_hbm, code_ref),
                (tgt_hbm, tgt_ref),
                (pos_hbm, pos_ref),
                (lr_hbm, lr_ref),
                (gr_hbm, gr_ref),
                (rg_hbm, rg_ref),
                (gp_hbm, gp_ref),
                (coup_hbm, coup_ref),
            )
        )
    ]
    for copy in small:
        copy.start()
    loads = []
    for y in range(ny):
        loads.append(
            pltpu.make_async_copy(
                fields_ref.at[:, :, y, :], q.at[pl.ds(0, nf), y + 3], in_sem.at[3 * y]
            )
        )
        loads.append(
            pltpu.make_async_copy(vel_ref.at[1, :, y, :], q.at[nf, y + 3], in_sem.at[3 * y + 1])
        )
        loads.append(
            pltpu.make_async_copy(vel_ref.at[0, :, y, :], ux.at[y], in_sem.at[3 * y + 2])
        )
    for copy in loads:
        copy.start()

    for copy in small:
        copy.wait()
    code = code_ref[0]
    target = tgt_ref[0]
    for r in range(3):
        vals[pl.ds(r, 1), :] = pos_ref[r, 0]
    vals[pl.ds(3, 1), :] = lr_ref[0]
    vals[pl.ds(4, 1), :] = gr_ref[0]
    vals[pl.ds(5, 1), :] = rg_ref[0]
    vals[pl.ds(6, 1), :] = gp_ref[0]
    vals[pl.ds(7, 1), :] = (target + 1).astype(f32)
    parts = split3_rows(vals[...])
    row16 = lax.broadcasted_iota(jnp.int32, (16, slots), 0)
    moves = jnp.where((row16 == code) & (row16 != 4) & (row16 < 9), 1.0, 0.0).astype(f32)
    chunks = slots // 128
    stacked = jnp.concatenate(
        [moves[:, 128 * k : 128 * (k + 1)] for k in range(chunks)], axis=0
    )
    upper = lax.broadcasted_iota(jnp.int32, (128, 128), 0) < lax.broadcasted_iota(
        jnp.int32, (128, 128), 1
    )
    before = dot(
        stacked.astype(jnp.bfloat16), jnp.where(upper, 1.0, 0.0).astype(jnp.bfloat16), False
    )
    offset = jnp.zeros((16, 1), f32)
    ranks = []
    for k in range(chunks):
        chunk = stacked[16 * k : 16 * (k + 1)]
        ranks.append(
            jnp.sum(chunk * (before[16 * k : 16 * (k + 1)] + offset), axis=0, keepdims=True)
        )
        offset = offset + jnp.sum(chunk, axis=1, keepdims=True)
    rank = jnp.concatenate(ranks, axis=1)
    row128 = lax.broadcasted_iota(jnp.int32, (128, slots), 0)
    pick = jnp.where(row128.astype(f32) == rank, 1.0, 0.0).astype(jnp.bfloat16)
    masked = jnp.concatenate([jnp.where(code == c, parts, 0.0) for c in DIRS], axis=0)
    boxes = dot(masked.astype(jnp.bfloat16), pick, True)
    for n in range(8):
        outbox[n] = (
            boxes[24 * n : 24 * n + 8] + boxes[24 * n + 8 : 24 * n + 16]
        ) + boxes[24 * n + 16 : 24 * n + 24]

    half = nz * ny // 128
    band = ny // half
    width = 2 * nx
    lanes_at_once = 3
    tiles = slots // 256

    def face_rows(buf, first, count, f, z):
        rows_q = [buf[f, first + i, z] for i in range(count + 5)]
        flux = [q[nf, first + i, z] * rows_q[i] for i in range(count + 5)]
        dq = [rows_q[i + 1] - rows_q[i] for i in range(count + 4)]
        df = [flux[i + 1] - flux[i] for i in range(count + 4)]
        for j in range(count):
            yface[f, first + j, z] = face_flux(
                dq[j : j + 5], df[j : j + 5], flux[j + 2] + flux[j + 3], topy[first + j, z]
            )

    def y_tops(first, count):
        for k in range(first, first + count):
            topy[k] = split_max([q[nf, k + i] for i in range(6)])

    def x_tops(blocks):
        for h in range(half):
            for b in blocks:
                topx[h, pl.ds(8 * b, 8)] = split_max(
                    [qt[nf, h, pl.ds(8 * b + 5 + i, 8)] for i in range(6)]
                )

    def x_cells(buf, f, h, blocks, dq_s, df_s, pair_s):
        for b in blocks:
            at, after = pl.ds(8 * b, 8), pl.ds(8 * b + 1, 8)
            here, there = buf[f, h, at], buf[f, h, after]
            flux_here, flux_there = qt[nf, h, at] * here, qt[nf, h, after] * there
            dq_s[at] = there - here
            df_s[at] = flux_there - flux_here
            pair_s[at] = flux_there + flux_here

    def x_faces(f, h, blocks, dq_s, df_s, pair_s):
        for b in blocks:
            dq = [dq_s[pl.ds(8 * b + 5 + i, 8)] for i in range(5)]
            df = [df_s[pl.ds(8 * b + 5 + i, 8)] for i in range(5)]
            xface[f, h, pl.ds(8 * b, 8)] = face_flux(
                dq, df, pair_s[pl.ds(8 * b + 7, 8)], topx[h, pl.ds(8 * b, 8)]
            )

    last = nx // 8

    def halves(h):
        return pl.ds(pl.multiple_of(h * 8, 8), 8)

    def inner_columns(buf, buft):
        def body(k, carry):
            for j in range(lanes_at_once):
                n = k * lanes_at_once + j
                f, h = n // half, n % half
                work = (dq_s.at[j], df_s.at[j], pair_s.at[j])
                x_cells(buft, f, h, range(1, last + 1), *work)
                x_faces(f, h, range(1, last - 1), *work)
                face_rows(buf, 3, ny - 5, f, halves(h))
            return carry

        lax.fori_loop(0, nf * half // lanes_at_once, body, 0)

    def outer_column(buf, buft, f, h, slot):
        work = (dq_s.at[slot], df_s.at[slot], pair_s.at[slot])
        x_cells(buft, f, h, (0, 1, 2, last - 1, last, last + 1), *work)
        x_faces(f, h, (0, last - 1, last), *work)
        blocks = [
            xface[f, h, pl.ds(8 * b + 1, 8)] - xface[f, h, pl.ds(8 * b, 8)] for b in range(last)
        ]
        turned = jnp.concatenate(blocks, axis=0).T
        dv[f, pl.ds(h * band, band)] = turned.reshape(band, nz, nx)
        face_rows(buf, 0, 3, f, halves(h))
        face_rows(buf, ny - 2, 3, f, halves(h))

    def outer_columns(buf, buft, y_rims, kind):
        sums = []
        for p in range(pieces):
            if p:
                for c, src, dst in y_rims[p]:
                    recv(kind + p, c, src, dst)
            for n in range(p * tiles // pieces, (p + 1) * tiles // pieces):
                sums.append(sample_tile(n))
            for n in range(p * group_of * half, (p + 1) * group_of * half):
                outer_column(buf, buft, n // half, n % half, n % 4)
        return jnp.concatenate(sums, axis=1)

    def turn(value):
        return value.reshape(128, nx).T

    def pack_rims(buf, count, packed):
        for f in range(count):
            for h in range(half):
                to = pl.ds(3 * (f * half + h), 3)
                packed[0, to] = buf[f, h, pl.ds(8, 3)]
                packed[1, to] = buf[f, h, pl.ds(nx + 5, 3)]

    def unpack_rims(buf, count, got):
        for f in range(count):
            for h in range(half):
                at = pl.ds(3 * (f * half + h), 3)
                buf[f, h, pl.ds(nx + 8, 3)] = got[0, at]
                buf[f, h, pl.ds(5, 3)] = got[1, at]

    wx[pl.ds(nx, nx)] = jnp.zeros((nx, slots), jnp.bfloat16)
    wx[pl.ds(width + nx, nx)] = jnp.zeros((nx, slots), jnp.bfloat16)
    wx[pl.ds(2 * width + nx, nx)] = jnp.zeros((nx, slots), jnp.bfloat16)
    tb[...] = jnp.zeros(tb.shape, f32)

    for copy in loads:
        copy.wait()
    for h in range(half):
        for f in range(nf):
            qt[f, h, pl.ds(8, nx)] = turn(q[f, pl.ds(3 + h * band, band)])
        qt[nf, h, pl.ds(8, nx)] = turn(ux[pl.ds(h * band, band)])
    pack_rims(qt, nf + 1, pk)
    y_tops(3, ny - 5)
    x_tops(range(1, last - 1))

    pl.semaphore_wait(barrier, neighbours)
    for c, src, dst in bubble_msgs:
        send(0, c, src, dst)
    for c, src, dst in y_speed:
        send(8, c, src, dst)
    for c, src, dst in y_rims0[0]:
        send(5, c, src, dst)
    for c, src, dst in rims0:
        send(1, c, src, dst)
    for p in range(1, pieces):
        for c, src, dst in y_rims0[p]:
            send(5 + p, c, src, dst)

    inner_columns(q, qt)

    def homes_of(values):
        slot = values[7:8].astype(jnp.int32) - 1
        slot_hi = slot >> 7
        slot_lo = slot & 127
        total = values.shape[1]
        place = jnp.where(
            lax.broadcasted_iota(jnp.int32, (128, total), 0) == slot_lo, 1.0, 0.0
        ).astype(jnp.bfloat16)
        parts = split3_rows(values)
        spread = jnp.concatenate(
            [jnp.where(slot_hi == h, parts, 0.0) for h in range(chunks)], axis=0
        )
        return dot(spread.astype(jnp.bfloat16), place, True)

    home_s[...] = homes_of(jnp.where(code == 4, vals[...], 0.0))
    for c, src, dst in bubble_msgs:
        recv(0, c, src, dst)
    homes = home_s[...] + homes_of(jnp.concatenate([inbox[n] for n in range(8)], axis=1))
    bubbles = jnp.concatenate(
        [
            (homes[24 * h : 24 * h + 8] + homes[24 * h + 8 : 24 * h + 16])
            + homes[24 * h + 16 : 24 * h + 24]
            for h in range(chunks)
        ],
        axis=1,
    )
    occupied = jnp.where(bubbles[7:8] > 0.5, 1.0, 0.0)
    local_x = bubbles[0:1] - (me_x * nx).astype(f32)
    local_y = bubbles[1:2] - (me_y * ny).astype(f32)

    def put_weight(row, first, count):
        cell = first + lax.broadcasted_iota(jnp.int32, (count, slots), 0)
        hi, lo = split2(tent(local_x - (cell.astype(f32) + 0.5)))
        wx[pl.ds(row, count)] = hi
        wx[pl.ds(width + row, count)] = hi
        wx[pl.ds(2 * width + row, count)] = lo

    put_weight(0, 0, nx)
    put_weight(nx, nx, 16)
    put_weight(width - 16, -16, 16)
    z_dist = jnp.abs(
        bubbles[2:3] - (lax.broadcasted_iota(jnp.int32, (nz, slots), 0).astype(f32) + 0.5)
    )
    weight_z = tent(jnp.minimum(z_dist, nz - z_dist))
    for ye in range(ny + 4):
        wzy[pl.ds(ye * nz, nz)] = weight_z * tent(local_y - (ye - 1.5))

    rows = (ny + 4) * nz
    step_rows = rows // 4

    def pack_rows(rows):
        packed = jnp.zeros((nz, nx), f32)
        for y, row in rows:
            packed = jnp.where(group == y, pltpu.roll(row, (8 * y + 3) % nx, 1), packed)
        return packed

    def sample_tile(n):
        at = pl.ds(256 * n, 256)
        prod = dot(samp[...], wx[:, at], False) * wzy[:, at]
        part = prod[0:8]
        for k in range(1, rows // 8):
            part = part + prod[8 * k : 8 * (k + 1)]
        return jnp.sum(part, axis=0, keepdims=True)

    def load_parts(volume):
        for k in range(4):
            at = pl.ds(k * step_rows, step_rows)
            hi, lo = split2(wzy[at] * volume)
            part_s[at] = hi
            part_s[pl.ds(rows + k * step_rows, step_rows)] = lo

    def deposit_product(at):
        both = dot(part_s[:, at], wx[pl.ds(0, width), at], True)
        return (both[:rows] + both[rows:]) + dot(
            part_s[pl.ds(0, rows), at], wx[pl.ds(2 * width, width), at], True
        )

    def send_smear(s, d):
        rims = []
        for r in range(ny + 4):
            dep[s, r] = d[r * nz : (r + 1) * nz, :nx]
            rims.append(d[r * nz : (r + 1) * nz, nx:])
        depx[s] = pack_rows([(y, rims[y + 2]) for y in range(ny)])
        depc[s] = pack_rows(
            [(0, rims[ny + 2]), (1, rims[ny + 3]), (ny - 2, rims[0]), (ny - 1, rims[1])]
        )
        for c, src, dst in smears[s]:
            send(2 + s, c, src, dst)

    def gather_smear(s):
        for c, src, dst in smears[s]:
            recv(2 + s, c, src, dst)
        low = lane < nx // 2
        from_right = dx_in[s, 0] + jnp.where(low, dc_in[s, 1], dc_in[s, 0])
        from_left = dx_in[s, 1] + jnp.where(low, dc_in[s, 3], dc_in[s, 2])
        return jnp.where(sub >= 3, from_left, from_right)

    def smear_row(s, merged, y):
        edge = (lane < 2) | (lane >= nx - 2)
        total_row = dep[s, y + 2] + jnp.where(
            edge, pltpu.roll(merged, (nx - 8 * y - 3) % nx, 1), 0.0
        )
        if y < 2:
            total_row = total_row + dy_in[s, 1, y]
        if y >= ny - 2:
            total_row = total_row + dy_in[s, 0, y - (ny - 2)]
        return total_row

    def put_sample(row, col, value):
        hi, lo = split2(value)
        count = value.shape[0]
        samp[pl.ds(row, count), pl.ds(col, nx)] = hi
        samp[pl.ds(row, count), pl.ds(width + col, nx)] = lo
        samp[pl.ds(row, count), pl.ds(2 * width + col, nx)] = hi

    def fill_sample(buf, buft, corner):
        for ye in range(ny + 4):
            put_sample(ye * nz, 0, buf[0, ye + 1])
        lanes = lax.broadcasted_iota(jnp.int32, (3, 128), 1)
        top = lanes >= 128 - 2 * nz
        final = 3 * (half - 1)
        for h in range(half):
            tb[h, pl.ds(0, 3)] = buft[0, h, pl.ds(nx + 8, 3)]
            tb[h, pl.ds(nx - 3, 3)] = buft[0, h, pl.ds(5, 3)]
        tb[half, pl.ds(0, 3)] = jnp.where(top, corner[1, pl.ds(final, 3)], corner[0, pl.ds(0, 3)])
        tb[half, pl.ds(nx - 3, 3)] = jnp.where(
            top, corner[3, pl.ds(final, 3)], corner[2, pl.ds(0, 3)]
        )
        for h in range(half):
            put_sample(2 * nz + 128 * h, nx, tb[h].T)
        turned = tb[half].T
        put_sample(0, nx, turned[128 - 2 * nz :])
        put_sample((ny + 2) * nz, nx, turned[: 2 * nz])

    rest_log = bubbles[3:4] + bubbles[5:6]
    pressure_gas = bubbles[6:7]

    def rate_of(s, w, sampled_field):
        gap = (
            pressure_gas * jnp.exp(-3.0 * (s - rest_log)) - 1.0 - 0.5 * sampled_field - 0.2 * w
        )
        return gap * jnp.exp(-2.0 * s) - 2.5 * w * w

    def volume_of(s, w):
        return occupied * four_pi * jnp.exp(3.0 * s) * w

    s_zero, w_zero = bubbles[3:4], bubbles[4:5]
    load_parts(volume_of(s_zero, w_zero))
    send_smear(0, deposit_product(pl.ds(0, slots)))

    for c, src, dst in y_speed:
        recv(8, c, src, dst)
    for c, src, dst in rims0:
        recv(1, c, src, dst)
    for c, src, dst in y_rims0[0]:
        recv(5, c, src, dst)
    unpack_rims(qt, nf + 1, pk_in)
    fill_sample(q, qt, c_in)
    y_tops(0, 3)
    y_tops(ny - 2, 3)
    x_tops((0, last - 1, last))
    sampled = outer_columns(q, qt, y_rims0, 5)
    s_one = s_zero + time_step * w_zero
    w_one = w_zero + time_step * rate_of(s_zero, w_zero, sampled)
    load_parts(volume_of(s_one, w_one))
    send_smear(1, deposit_product(pl.ds(0, slots)))

    merged = gather_smear(0)

    def first_section(y):
        source = time_step * smear_row(0, merged, y)
        for f in range(nf):
            div = dv[f, y] + (yface[f, y + 1] - yface[f, y])
            q1[f, y + 3] = (q[f, y + 3] - (time_step * flux_unit) * div) + coup_ref[f] * source

    outermost = [0, 1, 2, ny - 3, ny - 2, ny - 1]
    for y in outermost:
        first_section(y)
    for p in range(pieces):
        for c, src, dst in y_rims1[p]:
            send(9 + p, c, src, dst)
    for y in range(3, ny - 3):
        first_section(y)
    for h in range(half):
        for f in range(nf):
            qt1[f, h, pl.ds(8, nx)] = turn(q1[f, pl.ds(3 + h * band, band)])
    pack_rims(qt1, nf, pk1)
    for c, src, dst in rims1:
        send(4, c, src, dst)

    inner_columns(q1, qt1)
    for c, src, dst in rims1:
        recv(4, c, src, dst)
    for c, src, dst in y_rims1[0]:
        recv(9, c, src, dst)
    unpack_rims(qt1, nf, pk1_in)
    fill_sample(q1, qt1, c1_in)
    rate_two = rate_of(s_one, w_one, outer_columns(q1, qt1, y_rims1, 9))
    s_two = 0.5 * s_zero + 0.5 * (s_one + time_step * w_one)
    w_two = 0.5 * w_zero + 0.5 * (w_one + time_step * rate_two)
    bub_ref[0, 0] = s_two * occupied
    bub_ref[1, 0] = w_two * occupied
    merged1 = gather_smear(1)
    for y in range(ny):
        source = (0.5 * time_step) * smear_row(1, merged1, y)
        for f in range(nf):
            div = dv[f, y] + (yface[f, y + 1] - yface[f, y])
            out_ref[f, y] = (
                0.5 * (q[f, y + 3] + q1[f, y + 3]) - (0.5 * time_step * flux_unit) * div
            ) + coup_ref[f] * source

    for kind, msgs in ((0, bubble_msgs), (1, rims0), (2, smears[0]), (3, smears[1]), (4, rims1),
                       *((5 + p, y_rims0[p]) for p in range(pieces)), (8, y_speed),
                       *((9 + p, y_rims1[p]) for p in range(pieces))):
        for c, src, dst in msgs:
            sent(kind, c, src, dst)


def write_out(fields_ref, bubbles_ref, out_ref, bub_ref, sem):
    ny = fields_ref.shape[1]
    copies = [pltpu.make_async_copy(bubbles_ref, bub_ref, sem.at[ny])]
    for y in range(ny):
        copies.append(pltpu.make_async_copy(fields_ref.at[:, y], out_ref.at[:, :, y, :], sem.at[y]))
    for copy in copies:
        copy.start()
    for copy in copies:
        copy.wait()


def shards(n_gx, n_gy, fields, velocity, coupling, positions, log_radius, growth, rest_gap,
           gas_pressure, move_codes, targets):
    nf, nz, ny, nx = fields.shape
    slots = move_codes.shape[2]
    vmem = pl.BlockSpec(memory_space=pltpu.VMEM)
    f32 = jnp.float32
    rows = (ny + 4) * nz
    half = nz * ny // 128
    deep = nx + 24
    packed = -(-3 * half * (nf + 1) // 8) * 8
    sc = lambda *shape: pltpu.VMEM(shape, f32)
    out, bub = pl.pallas_call(
        functools.partial(kernel, n_gx, n_gy, (nf, nz, ny, nx, slots)),
        out_shape=(
            pltpu.VMEM((nf, ny, nz, nx), f32),
            pltpu.VMEM((2, 1, 1, slots), f32),
        ),
        in_specs=[pl.BlockSpec(memory_space=pltpu.HBM)] * 10,
        out_specs=(vmem, vmem),
        scratch_shapes=[
            pltpu.SMEM((nf,), f32),
            sc(3, 1, 1, slots),
            sc(1, 1, slots),
            sc(1, 1, slots),
            sc(1, 1, slots),
            sc(1, 1, slots),
            pltpu.VMEM((1, 1, slots), jnp.int32),
            pltpu.VMEM((1, 1, slots), jnp.int32),
            pltpu.SemaphoreType.DMA((8,)),
            sc(nf + 1, ny + 6, nz, nx),
            sc(nf, ny + 6, nz, nx),
            sc(ny, nz, nx),
            sc(nf + 1, half, deep, 128),
            sc(nf, half, deep, 128),
            sc(ny + 1, nz, nx),
            sc(half, nx + 8, 128),
            sc(4, deep, 128),
            sc(4, deep, 128),
            sc(4, deep, 128),
            sc(nf, half, nx + 16, 128),
            sc(nf, ny, nz, nx),
            sc(2, packed, 128),
            sc(2, packed, 128),
            sc(4, 8, 128),
            sc(2, packed, 128),
            sc(2, packed, 128),
            sc(4, 8, 128),
            sc(half + 1, 128, 128),
            sc(8, 8, 128),
            sc(8, 8, 128),
            sc(8, slots),
            sc(24 * (slots // 128), 128),
            pltpu.VMEM((rows, 6 * nx), jnp.bfloat16),
            pltpu.VMEM((6 * nx, slots), jnp.bfloat16),
            sc(rows, slots),
            pltpu.VMEM((2 * rows, slots), jnp.bfloat16),
            sc(2, ny + 4, nz, nx),
            sc(2, nz, nx),
            sc(2, nz, nx),
            sc(2, 2, 2, nz, nx),
            sc(2, 2, nz, nx),
            sc(2, 4, nz, nx),
            sc(nf, ny + 1, nz, nx),
            pltpu.SemaphoreType.DMA((3 * ny,)),
            pltpu.SemaphoreType.DMA((12, 9)),
            pltpu.SemaphoreType.DMA((12, 9)),
        ],
        compiler_params=pltpu.CompilerParams(
            collective_id=0, has_side_effects=True
        ),
    )(fields, velocity, coupling, positions, log_radius, growth, rest_gap, gas_pressure,
      move_codes, targets)
    here = functools.partial(pltpu.with_memory_space_constraint, memory_space=pltpu.VMEM)
    return pl.pallas_call(
        write_out,
        out_shape=(
            jax.ShapeDtypeStruct((nf, nz, ny, nx), f32),
            jax.ShapeDtypeStruct((2, 1, 1, slots), f32),
        ),
        in_specs=[vmem, vmem],
        out_specs=(pl.BlockSpec(memory_space=pl.ANY), pl.BlockSpec(memory_space=pl.ANY)),
        scratch_shapes=[pltpu.SemaphoreType.DMA((ny + 1,))],
    )(here(out), here(bub))


def solution(mesh):
    placed = (
        P(None, None, "gy", "gx"),
        P(None, None, "gy", "gx"),
        P(),
        P(None, "gx", "gy", None),
        P("gx", "gy", None),
        P("gx", "gy", None),
        P("gx", "gy", None),
        P("gx", "gy", None),
        P("gx", "gy", None),
        P("gx", "gy", None),
    )
    return jax.shard_map(
        functools.partial(shards, mesh.shape["gx"], mesh.shape["gy"]),
        mesh=mesh,
        in_specs=placed,
        out_specs=(P(None, None, "gy", "gx"), P(None, "gx", "gy", None)),
        check_vma=False,
    )
```

```python
import functools
import math

import jax
import jax.numpy as jnp
from jax import lax
from jax.experimental import pallas as pl
from jax.experimental.pallas import tpu as pltpu
from jax.sharding import PartitionSpec as P

time_step = 0.2
four_pi = 4.0 * math.pi
smooth_eps = 3e-6
flux_unit = 1.0 / 12.0

DIRS = [c for c in range(9) if c != 4]
X_DIRS = (1, 7)
Y_DIRS = (3, 5)
DIAG = (0, 2, 6, 8)
pieces = 3


def weno_side(d1, d2, d3, d4):
    t1 = d2 - d1
    t2 = d3 - d2
    t3 = d4 - d3
    x = 0.75 * d2
    y = 0.75 * d3
    near = x * d2 + smooth_eps
    b0 = t1 * (t1 + x) + near
    b1 = t2 * (t2 + x) + near
    b2 = t3 * (t3 - y) + (y * d3 + smooth_eps)
    j1 = b0 / b1
    j2 = b0 / b2
    w2 = (1.5 * j2) * j2
    w1 = (3.0 * j1) * j1
    return ((t1 - t2) + w2 * (t2 - t3)) / (w2 + w1 + 0.5) - t2


def face_flux(dq, df, pair, top):
    p = [top * d for d in dq]
    r = [df[i] + p[i] for i in range(4)]
    l = [df[i + 1] - p[i + 1] for i in range(4)]
    return 6.0 * pair + (weno_side(*r) - weno_side(l[3], l[2], l[1], l[0]))


def split_max(u):
    a = [jnp.abs(v) for v in u]
    return jnp.maximum(
        jnp.maximum(jnp.maximum(a[0], a[1]), jnp.maximum(a[2], a[3])), jnp.maximum(a[4], a[5])
    )


def split2(v):
    hi = v.astype(jnp.bfloat16)
    lo = (v - hi.astype(jnp.float32)).astype(jnp.bfloat16)
    return hi, lo


def split3_rows(v):
    hi = v.astype(jnp.bfloat16).astype(jnp.float32)
    rest = v - hi
    mid = rest.astype(jnp.bfloat16).astype(jnp.float32)
    return jnp.concatenate([hi, mid, rest - mid], axis=0)


def tent(d):
    return jnp.maximum(0.0, 0.5 - jnp.abs(0.25 * d))


def dot(a, b, trans):
    dims = (((1,), (1,)), ((), ())) if trans else (((1,), (0,)), ((), ()))
    return lax.dot_general(a, b, dims, preferred_element_type=jnp.float32)


def kernel(
    n_gx,
    n_gy,
    dims,
    fields_ref,
    vel_ref,
    coup_hbm,
    pos_hbm,
    lr_hbm,
    gr_hbm,
    rg_hbm,
    gp_hbm,
    code_hbm,
    tgt_hbm,
    out_ref,
    bub_ref,
    coup_ref,
    pos_ref,
    lr_ref,
    gr_ref,
    rg_ref,
    gp_ref,
    code_ref,
    tgt_ref,
    small_sem,
    q,
    q1,
    ux,
    qt,
    qt1,
    topy,
    topx,
    dq_s,
    df_s,
    pair_s,
    xface,
    dv,
    pk,
    pk_in,
    c_in,
    pk1,
    pk1_in,
    c1_in,
    tb,
    outbox,
    inbox,
    vals,
    home_s,
    samp,
    wx,
    wzy,
    part_s,
    dep,
    depx,
    depc,
    dy_in,
    dx_in,
    dc_in,
    yface,
    in_sem,
    send_sem,
    recv_sem,
):
    nf, nz, ny, nx, slots = dims
    f32 = jnp.float32
    me_x = lax.axis_index("gx")
    me_y = lax.axis_index("gy")
    lane = lax.broadcasted_iota(jnp.int32, (nz, nx), 1)
    group = lane // 8
    sub = lane % 8

    def inside(c, sign):
        a, b = sign * (c // 3 - 1), sign * (c % 3 - 1)
        ok = None
        for pos, step, count in ((me_x, a, n_gx), (me_y, b, n_gy)):
            cond = None
            if step == 1:
                cond = pos < count - 1
            elif step == -1:
                cond = pos > 0
            if cond is not None:
                ok = cond if ok is None else jnp.logical_and(ok, cond)
        return ok

    def desc(kind, c, src, dst):
        return pltpu.make_async_remote_copy(
            src_ref=src,
            dst_ref=dst,
            send_sem=send_sem.at[kind, c],
            recv_sem=recv_sem.at[kind, c],
            device_id=(me_x + (c // 3 - 1), me_y + (c % 3 - 1)),
            device_id_type=pl.DeviceIdType.MESH,
        )

    def send(kind, c, src, dst):
        @pl.when(inside(c, 1))
        def _():
            desc(kind, c, src, dst).start()

    def sent(kind, c, src, dst):
        @pl.when(inside(c, 1))
        def _():
            desc(kind, c, src, dst).wait_send()

    def recv(kind, c, src, dst):
        @pl.when(inside(c, -1))
        def _():
            desc(kind, c, src, dst).wait_recv()

        @pl.when(jnp.logical_not(inside(c, -1)))
        def _():
            dst[...] = jnp.zeros(dst.shape, f32)

    def y_msgs(buf, first, count):
        f = pl.ds(first, count)
        yield 3, buf.at[f, pl.ds(3, 3)], buf.at[f, pl.ds(ny + 3, 3)]
        yield 5, buf.at[f, pl.ds(ny, 3)], buf.at[f, pl.ds(0, 3)]

    def rim_msgs(packed, packed_in, corner_in):
        for n, c in enumerate(X_DIRS):
            yield c, packed.at[n], packed_in.at[n]
        for n, c in enumerate(DIAG):
            yield c, packed.at[n // 2, pl.ds(0, 8)], corner_in.at[n]

    def smear_msgs(s):
        yield 3, dep.at[s, pl.ds(0, 2)], dy_in.at[s, 0]
        yield 5, dep.at[s, pl.ds(ny + 2, 2)], dy_in.at[s, 1]
        for n, c in enumerate(X_DIRS):
            yield c, depx.at[s], dx_in.at[s, n]
        for n, c in enumerate(DIAG):
            yield c, depc.at[s], dc_in.at[s, n]

    bubble_msgs = [(c, outbox.at[n], inbox.at[n]) for n, c in enumerate(DIRS)]
    rims0 = list(rim_msgs(pk, pk_in, c_in))
    rims1 = list(rim_msgs(pk1, pk1_in, c1_in))
    group_of = nf // pieces
    y_rims0 = [list(y_msgs(q, p * group_of, group_of)) for p in range(pieces)]
    y_rims1 = [list(y_msgs(q1, p * group_of, group_of)) for p in range(pieces)]
    y_speed = list(y_msgs(q, nf, 1))
    smears = [list(smear_msgs(0)), list(smear_msgs(1))]

    barrier = pltpu.get_barrier_semaphore()
    neighbours = jnp.int32(0)
    for c in DIRS:
        ok = inside(c, 1)

        @pl.when(ok)
        def _():
            pl.semaphore_signal(
                barrier,
                inc=1,
                device_id=(me_x + (c // 3 - 1), me_y + (c % 3 - 1)),
                device_id_type=pl.DeviceIdType.MESH,
            )

        neighbours = neighbours + ok.astype(jnp.int32)

    small = [
        pltpu.make_async_copy(src, dst, small_sem.at[n])
        for n, (src, dst) in enumerate(
            (
                (code_hbm, code_ref),
                (tgt_hbm, tgt_ref),
                (pos_hbm, pos_ref),
                (lr_hbm, lr_ref),
                (gr_hbm, gr_ref),
                (rg_hbm, rg_ref),
                (gp_hbm, gp_ref),
                (coup_hbm, coup_ref),
            )
        )
    ]
    for copy in small:
        copy.start()
    loads = []
    for y in range(ny):
        loads.append(
            pltpu.make_async_copy(
                fields_ref.at[:, :, y, :], q.at[pl.ds(0, nf), y + 3], in_sem.at[3 * y]
            )
        )
        loads.append(
            pltpu.make_async_copy(vel_ref.at[1, :, y, :], q.at[nf, y + 3], in_sem.at[3 * y + 1])
        )
        loads.append(
            pltpu.make_async_copy(vel_ref.at[0, :, y, :], ux.at[y], in_sem.at[3 * y + 2])
        )
    for copy in loads:
        copy.start()

    for copy in small:
        copy.wait()
    code = code_ref[0]
    target = tgt_ref[0]
    for r in range(3):
        vals[pl.ds(r, 1), :] = pos_ref[r, 0]
    vals[pl.ds(3, 1), :] = lr_ref[0]
    vals[pl.ds(4, 1), :] = gr_ref[0]
    vals[pl.ds(5, 1), :] = rg_ref[0]
    vals[pl.ds(6, 1), :] = gp_ref[0]
    vals[pl.ds(7, 1), :] = (target + 1).astype(f32)
    parts = split3_rows(vals[...])
    row16 = lax.broadcasted_iota(jnp.int32, (16, slots), 0)
    moves = jnp.where((row16 == code) & (row16 != 4) & (row16 < 9), 1.0, 0.0).astype(f32)
    chunks = slots // 128
    stacked = jnp.concatenate(
        [moves[:, 128 * k : 128 * (k + 1)] for k in range(chunks)], axis=0
    )
    upper = lax.broadcasted_iota(jnp.int32, (128, 128), 0) < lax.broadcasted_iota(
        jnp.int32, (128, 128), 1
    )
    before = dot(
        stacked.astype(jnp.bfloat16), jnp.where(upper, 1.0, 0.0).astype(jnp.bfloat16), False
    )
    offset = jnp.zeros((16, 1), f32)
    ranks = []
    for k in range(chunks):
        chunk = stacked[16 * k : 16 * (k + 1)]
        ranks.append(
            jnp.sum(chunk * (before[16 * k : 16 * (k + 1)] + offset), axis=0, keepdims=True)
        )
        offset = offset + jnp.sum(chunk, axis=1, keepdims=True)
    rank = jnp.concatenate(ranks, axis=1)
    row128 = lax.broadcasted_iota(jnp.int32, (128, slots), 0)
    pick = jnp.where(row128.astype(f32) == rank, 1.0, 0.0).astype(jnp.bfloat16)
    masked = jnp.concatenate([jnp.where(code == c, parts, 0.0) for c in DIRS], axis=0)
    boxes = dot(masked.astype(jnp.bfloat16), pick, True)
    for n in range(8):
        outbox[n] = (
            boxes[24 * n : 24 * n + 8] + boxes[24 * n + 8 : 24 * n + 16]
        ) + boxes[24 * n + 16 : 24 * n + 24]

    half = nz * ny // 128
    band = ny // half
    width = 2 * nx
    lanes_at_once = 3
    tiles = slots // 256

    def face_rows(buf, first, count, f, z):
        rows_q = [buf[f, first + i, z] for i in range(count + 5)]
        flux = [q[nf, first + i, z] * rows_q[i] for i in range(count + 5)]
        dq = [rows_q[i + 1] - rows_q[i] for i in range(count + 4)]
        df = [flux[i + 1] - flux[i] for i in range(count + 4)]
        for j in range(count):
            yface[f, first + j, z] = face_flux(
                dq[j : j + 5], df[j : j + 5], flux[j + 2] + flux[j + 3], topy[first + j, z]
            )

    def y_tops(first, count):
        for k in range(first, first + count):
            topy[k] = split_max([q[nf, k + i] for i in range(6)])

    def x_tops(blocks):
        for h in range(half):
            for b in blocks:
                topx[h, pl.ds(8 * b, 8)] = split_max(
                    [qt[nf, h, pl.ds(8 * b + 5 + i, 8)] for i in range(6)]
                )

    def x_cells(buf, f, h, blocks, dq_s, df_s, pair_s):
        for b in blocks:
            at, after = pl.ds(8 * b, 8), pl.ds(8 * b + 1, 8)
            here, there = buf[f, h, at], buf[f, h, after]
            flux_here, flux_there = qt[nf, h, at] * here, qt[nf, h, after] * there
            dq_s[at] = there - here
            df_s[at] = flux_there - flux_here
            pair_s[at] = flux_there + flux_here

    def x_faces(f, h, blocks, dq_s, df_s, pair_s):
        for b in blocks:
            dq = [dq_s[pl.ds(8 * b + 5 + i, 8)] for i in range(5)]
            df = [df_s[pl.ds(8 * b + 5 + i, 8)] for i in range(5)]
            xface[f, h, pl.ds(8 * b, 8)] = face_flux(
                dq, df, pair_s[pl.ds(8 * b + 7, 8)], topx[h, pl.ds(8 * b, 8)]
            )

    last = nx // 8

    def halves(h):
        return pl.ds(pl.multiple_of(h * 8, 8), 8)

    def inner_columns(buf, buft):
        def body(k, carry):
            for j in range(lanes_at_once):
                n = k * lanes_at_once + j
                f, h = n // half, n % half
                work = (dq_s.at[j], df_s.at[j], pair_s.at[j])
                x_cells(buft, f, h, range(1, last + 1), *work)
                x_faces(f, h, range(1, last - 1), *work)
                face_rows(buf, 3, ny - 5, f, halves(h))
            return carry

        lax.fori_loop(0, nf * half // lanes_at_once, body, 0)

    def outer_column(buf, buft, f, h, slot):
        work = (dq_s.at[slot], df_s.at[slot], pair_s.at[slot])
        x_cells(buft, f, h, (0, 1, 2, last - 1, last, last + 1), *work)
        x_faces(f, h, (0, last - 1, last), *work)
        blocks = [
            xface[f, h, pl.ds(8 * b + 1, 8)] - xface[f, h, pl.ds(8 * b, 8)] for b in range(last)
        ]
        turned = jnp.concatenate(blocks, axis=0).T
        dv[f, pl.ds(h * band, band)] = turned.reshape(band, nz, nx)

    def outer_rows(buf, y_rims, kind, p):
        if p:
            for c, src, dst in y_rims[p]:
                recv(kind + p, c, src, dst)
        for n in range(p * group_of * half, (p + 1) * group_of * half):
            face_rows(buf, 0, 3, n // half, halves(n % half))
            face_rows(buf, ny - 2, 3, n // half, halves(n % half))

    def outer_columns(buf, buft, y_rims, kind, rows_too):
        sums = []
        for p in range(pieces):
            if rows_too:
                outer_rows(buf, y_rims, kind, p)
            for n in range(p * tiles // pieces, (p + 1) * tiles // pieces):
                sums.append(sample_tile(n))
            for n in range(p * group_of * half, (p + 1) * group_of * half):
                outer_column(buf, buft, n // half, n % half, n % 4)
        return jnp.concatenate(sums, axis=1)

    def turn(value):
        return value.reshape(128, nx).T

    def pack_rims(buf, count, packed):
        for f in range(count):
            for h in range(half):
                to = pl.ds(3 * (f * half + h), 3)
                packed[0, to] = buf[f, h, pl.ds(8, 3)]
                packed[1, to] = buf[f, h, pl.ds(nx + 5, 3)]

    def unpack_rims(buf, count, got):
        for f in range(count):
            for h in range(half):
                at = pl.ds(3 * (f * half + h), 3)
                buf[f, h, pl.ds(nx + 8, 3)] = got[0, at]
                buf[f, h, pl.ds(5, 3)] = got[1, at]

    wx[pl.ds(nx, nx)] = jnp.zeros((nx, slots), jnp.bfloat16)
    wx[pl.ds(width + nx, nx)] = jnp.zeros((nx, slots), jnp.bfloat16)
    wx[pl.ds(2 * width + nx, nx)] = jnp.zeros((nx, slots), jnp.bfloat16)
    tb[...] = jnp.zeros(tb.shape, f32)

    for copy in loads:
        copy.wait()
    for h in range(half):
        for f in range(nf):
            qt[f, h, pl.ds(8, nx)] = turn(q[f, pl.ds(3 + h * band, band)])
        qt[nf, h, pl.ds(8, nx)] = turn(ux[pl.ds(h * band, band)])
    pack_rims(qt, nf + 1, pk)
    y_tops(3, ny - 5)
    x_tops(range(1, last - 1))

    pl.semaphore_wait(barrier, neighbours)
    for c, src, dst in bubble_msgs:
        send(0, c, src, dst)
    for c, src, dst in y_speed:
        send(8, c, src, dst)
    for c, src, dst in y_rims0[0]:
        send(5, c, src, dst)
    for c, src, dst in rims0:
        send(1, c, src, dst)
    for p in range(1, pieces):
        for c, src, dst in y_rims0[p]:
            send(5 + p, c, src, dst)

    inner_columns(q, qt)

    def homes_of(values):
        slot = values[7:8].astype(jnp.int32) - 1
        slot_hi = slot >> 7
        slot_lo = slot & 127
        total = values.shape[1]
        place = jnp.where(
            lax.broadcasted_iota(jnp.int32, (128, total), 0) == slot_lo, 1.0, 0.0
        ).astype(jnp.bfloat16)
        parts = split3_rows(values)
        spread = jnp.concatenate(
            [jnp.where(slot_hi == h, parts, 0.0) for h in range(chunks)], axis=0
        )
        return dot(spread.astype(jnp.bfloat16), place, True)

    home_s[...] = homes_of(jnp.where(code == 4, vals[...], 0.0))
    for c, src, dst in bubble_msgs:
        recv(0, c, src, dst)
    homes = home_s[...] + homes_of(jnp.concatenate([inbox[n] for n in range(8)], axis=1))
    bubbles = jnp.concatenate(
        [
            (homes[24 * h : 24 * h + 8] + homes[24 * h + 8 : 24 * h + 16])
            + homes[24 * h + 16 : 24 * h + 24]
            for h in range(chunks)
        ],
        axis=1,
    )
    occupied = jnp.where(bubbles[7:8] > 0.5, 1.0, 0.0)
    local_x = bubbles[0:1] - (me_x * nx).astype(f32)
    local_y = bubbles[1:2] - (me_y * ny).astype(f32)

    def put_weight(row, first, count):
        cell = first + lax.broadcasted_iota(jnp.int32, (count, slots), 0)
        hi, lo = split2(tent(local_x - (cell.astype(f32) + 0.5)))
        wx[pl.ds(row, count)] = hi
        wx[pl.ds(width + row, count)] = hi
        wx[pl.ds(2 * width + row, count)] = lo

    put_weight(0, 0, nx)
    put_weight(nx, nx, 16)
    put_weight(width - 16, -16, 16)
    z_dist = jnp.abs(
        bubbles[2:3] - (lax.broadcasted_iota(jnp.int32, (nz, slots), 0).astype(f32) + 0.5)
    )
    weight_z = tent(jnp.minimum(z_dist, nz - z_dist))
    for ye in range(ny + 4):
        wzy[pl.ds(ye * nz, nz)] = weight_z * tent(local_y - (ye - 1.5))

    rows = (ny + 4) * nz
    step_rows = rows // 4

    def pack_rows(rows):
        packed = jnp.zeros((nz, nx), f32)
        for y, row in rows:
            packed = jnp.where(group == y, pltpu.roll(row, (8 * y + 3) % nx, 1), packed)
        return packed

    def sample_tile(n):
        at = pl.ds(256 * n, 256)
        prod = dot(samp[...], wx[:, at], False) * wzy[:, at]
        part = prod[0:8]
        for k in range(1, rows // 8):
            part = part + prod[8 * k : 8 * (k + 1)]
        return jnp.sum(part, axis=0, keepdims=True)

    def load_parts(volume):
        for k in range(4):
            at = pl.ds(k * step_rows, step_rows)
            hi, lo = split2(wzy[at] * volume)
            part_s[at] = hi
            part_s[pl.ds(rows + k * step_rows, step_rows)] = lo

    def deposit_product(at):
        both = dot(part_s[:, at], wx[pl.ds(0, width), at], True)
        return (both[:rows] + both[rows:]) + dot(
            part_s[pl.ds(0, rows), at], wx[pl.ds(2 * width, width), at], True
        )

    def send_smear(s, d):
        rims = []
        for r in range(ny + 4):
            dep[s, r] = d[r * nz : (r + 1) * nz, :nx]
            rims.append(d[r * nz : (r + 1) * nz, nx:])
        depx[s] = pack_rows([(y, rims[y + 2]) for y in range(ny)])
        depc[s] = pack_rows(
            [(0, rims[ny + 2]), (1, rims[ny + 3]), (ny - 2, rims[0]), (ny - 1, rims[1])]
        )
        for c, src, dst in smears[s]:
            send(2 + s, c, src, dst)

    def gather_smear(s):
        for c, src, dst in smears[s]:
            recv(2 + s, c, src, dst)
        low = lane < nx // 2
        from_right = dx_in[s, 0] + jnp.where(low, dc_in[s, 1], dc_in[s, 0])
        from_left = dx_in[s, 1] + jnp.where(low, dc_in[s, 3], dc_in[s, 2])
        return jnp.where(sub >= 3, from_left, from_right)

    def smear_row(s, merged, y):
        edge = (lane < 2) | (lane >= nx - 2)
        total_row = dep[s, y + 2] + jnp.where(
            edge, pltpu.roll(merged, (nx - 8 * y - 3) % nx, 1), 0.0
        )
        if y < 2:
            total_row = total_row + dy_in[s, 1, y]
        if y >= ny - 2:
            total_row = total_row + dy_in[s, 0, y - (ny - 2)]
        return total_row

    def put_sample(row, col, value):
        hi, lo = split2(value)
        count = value.shape[0]
        samp[pl.ds(row, count), pl.ds(col, nx)] = hi
        samp[pl.ds(row, count), pl.ds(width + col, nx)] = lo
        samp[pl.ds(row, count), pl.ds(2 * width + col, nx)] = hi

    def fill_sample(buf, buft, corner):
        for ye in range(ny + 4):
            put_sample(ye * nz, 0, buf[0, ye + 1])
        lanes = lax.broadcasted_iota(jnp.int32, (3, 128), 1)
        top = lanes >= 128 - 2 * nz
        final = 3 * (half - 1)
        for h in range(half):
            tb[h, pl.ds(0, 3)] = buft[0, h, pl.ds(nx + 8, 3)]
            tb[h, pl.ds(nx - 3, 3)] = buft[0, h, pl.ds(5, 3)]
        tb[half, pl.ds(0, 3)] = jnp.where(top, corner[1, pl.ds(final, 3)], corner[0, pl.ds(0, 3)])
        tb[half, pl.ds(nx - 3, 3)] = jnp.where(
            top, corner[3, pl.ds(final, 3)], corner[2, pl.ds(0, 3)]
        )
        for h in range(half):
            put_sample(2 * nz + 128 * h, nx, tb[h].T)
        turned = tb[half].T
        put_sample(0, nx, turned[128 - 2 * nz :])
        put_sample((ny + 2) * nz, nx, turned[: 2 * nz])

    rest_log = bubbles[3:4] + bubbles[5:6]
    pressure_gas = bubbles[6:7]

    def rate_of(s, w, sampled_field):
        gap = (
            pressure_gas * jnp.exp(-3.0 * (s - rest_log)) - 1.0 - 0.5 * sampled_field - 0.2 * w
        )
        return gap * jnp.exp(-2.0 * s) - 2.5 * w * w

    def volume_of(s, w):
        return occupied * four_pi * jnp.exp(3.0 * s) * w

    s_zero, w_zero = bubbles[3:4], bubbles[4:5]
    load_parts(volume_of(s_zero, w_zero))
    send_smear(0, deposit_product(pl.ds(0, slots)))

    for c, src, dst in y_speed:
        recv(8, c, src, dst)
    for c, src, dst in rims0:
        recv(1, c, src, dst)
    for c, src, dst in y_rims0[0]:
        recv(5, c, src, dst)
    unpack_rims(qt, nf + 1, pk_in)
    fill_sample(q, qt, c_in)
    y_tops(0, 3)
    y_tops(ny - 2, 3)
    x_tops((0, last - 1, last))
    sampled = outer_columns(q, qt, y_rims0, 5, True)
    s_one = s_zero + time_step * w_zero
    w_one = w_zero + time_step * rate_of(s_zero, w_zero, sampled)
    load_parts(volume_of(s_one, w_one))
    send_smear(1, deposit_product(pl.ds(0, slots)))

    merged = gather_smear(0)

    def first_section(y):
        source = time_step * smear_row(0, merged, y)
        for f in range(nf):
            div = dv[f, y] + (yface[f, y + 1] - yface[f, y])
            q1[f, y + 3] = (q[f, y + 3] - (time_step * flux_unit) * div) + coup_ref[f] * source

    outermost = [0, 1, 2, ny - 3, ny - 2, ny - 1]
    for y in outermost:
        first_section(y)
    for p in range(pieces):
        for c, src, dst in y_rims1[p]:
            send(9 + p, c, src, dst)
    for y in range(3, ny - 3):
        first_section(y)
    for h in range(half):
        for f in range(nf):
            qt1[f, h, pl.ds(8, nx)] = turn(q1[f, pl.ds(3 + h * band, band)])
    pack_rims(qt1, nf, pk1)
    for c, src, dst in rims1:
        send(4, c, src, dst)

    inner_columns(q1, qt1)
    for c, src, dst in y_rims1[0]:
        recv(9, c, src, dst)
    for p in range(pieces):
        outer_rows(q1, y_rims1, 9, p)
    for c, src, dst in rims1:
        recv(4, c, src, dst)
    unpack_rims(qt1, nf, pk1_in)
    fill_sample(q1, qt1, c1_in)
    rate_two = rate_of(s_one, w_one, outer_columns(q1, qt1, y_rims1, 9, False))
    s_two = 0.5 * s_zero + 0.5 * (s_one + time_step * w_one)
    w_two = 0.5 * w_zero + 0.5 * (w_one + time_step * rate_two)
    bub_ref[0, 0] = s_two * occupied
    bub_ref[1, 0] = w_two * occupied
    merged1 = gather_smear(1)
    for y in range(ny):
        source = (0.5 * time_step) * smear_row(1, merged1, y)
        for f in range(nf):
            div = dv[f, y] + (yface[f, y + 1] - yface[f, y])
            out_ref[f, y] = (
                0.5 * (q[f, y + 3] + q1[f, y + 3]) - (0.5 * time_step * flux_unit) * div
            ) + coup_ref[f] * source

    for kind, msgs in ((0, bubble_msgs), (1, rims0), (2, smears[0]), (3, smears[1]), (4, rims1),
                       *((5 + p, y_rims0[p]) for p in range(pieces)), (8, y_speed),
                       *((9 + p, y_rims1[p]) for p in range(pieces))):
        for c, src, dst in msgs:
            sent(kind, c, src, dst)


def write_out(fields_ref, bubbles_ref, out_ref, bub_ref, sem):
    ny = fields_ref.shape[1]
    copies = [pltpu.make_async_copy(bubbles_ref, bub_ref, sem.at[ny])]
    for y in range(ny):
        copies.append(pltpu.make_async_copy(fields_ref.at[:, y], out_ref.at[:, :, y, :], sem.at[y]))
    for copy in copies:
        copy.start()
    for copy in copies:
        copy.wait()


def shards(n_gx, n_gy, fields, velocity, coupling, positions, log_radius, growth, rest_gap,
           gas_pressure, move_codes, targets):
    nf, nz, ny, nx = fields.shape
    slots = move_codes.shape[2]
    vmem = pl.BlockSpec(memory_space=pltpu.VMEM)
    f32 = jnp.float32
    rows = (ny + 4) * nz
    half = nz * ny // 128
    deep = nx + 24
    packed = -(-3 * half * (nf + 1) // 8) * 8
    sc = lambda *shape: pltpu.VMEM(shape, f32)
    out, bub = pl.pallas_call(
        functools.partial(kernel, n_gx, n_gy, (nf, nz, ny, nx, slots)),
        out_shape=(
            pltpu.VMEM((nf, ny, nz, nx), f32),
            pltpu.VMEM((2, 1, 1, slots), f32),
        ),
        in_specs=[pl.BlockSpec(memory_space=pltpu.HBM)] * 10,
        out_specs=(vmem, vmem),
        scratch_shapes=[
            pltpu.SMEM((nf,), f32),
            sc(3, 1, 1, slots),
            sc(1, 1, slots),
            sc(1, 1, slots),
            sc(1, 1, slots),
            sc(1, 1, slots),
            pltpu.VMEM((1, 1, slots), jnp.int32),
            pltpu.VMEM((1, 1, slots), jnp.int32),
            pltpu.SemaphoreType.DMA((8,)),
            sc(nf + 1, ny + 6, nz, nx),
            sc(nf, ny + 6, nz, nx),
            sc(ny, nz, nx),
            sc(nf + 1, half, deep, 128),
            sc(nf, half, deep, 128),
            sc(ny + 1, nz, nx),
            sc(half, nx + 8, 128),
            sc(4, deep, 128),
            sc(4, deep, 128),
            sc(4, deep, 128),
            sc(nf, half, nx + 16, 128),
            sc(nf, ny, nz, nx),
            sc(2, packed, 128),
            sc(2, packed, 128),
            sc(4, 8, 128),
            sc(2, packed, 128),
            sc(2, packed, 128),
            sc(4, 8, 128),
            sc(half + 1, 128, 128),
            sc(8, 8, 128),
            sc(8, 8, 128),
            sc(8, slots),
            sc(24 * (slots // 128), 128),
            pltpu.VMEM((rows, 6 * nx), jnp.bfloat16),
            pltpu.VMEM((6 * nx, slots), jnp.bfloat16),
            sc(rows, slots),
            pltpu.VMEM((2 * rows, slots), jnp.bfloat16),
            sc(2, ny + 4, nz, nx),
            sc(2, nz, nx),
            sc(2, nz, nx),
            sc(2, 2, 2, nz, nx),
            sc(2, 2, nz, nx),
            sc(2, 4, nz, nx),
            sc(nf, ny + 1, nz, nx),
            pltpu.SemaphoreType.DMA((3 * ny,)),
            pltpu.SemaphoreType.DMA((12, 9)),
            pltpu.SemaphoreType.DMA((12, 9)),
        ],
        compiler_params=pltpu.CompilerParams(
            collective_id=0, has_side_effects=True
        ),
    )(fields, velocity, coupling, positions, log_radius, growth, rest_gap, gas_pressure,
      move_codes, targets)
    here = functools.partial(pltpu.with_memory_space_constraint, memory_space=pltpu.VMEM)
    return pl.pallas_call(
        write_out,
        out_shape=(
            jax.ShapeDtypeStruct((nf, nz, ny, nx), f32),
            jax.ShapeDtypeStruct((2, 1, 1, slots), f32),
        ),
        in_specs=[vmem, vmem],
        out_specs=(pl.BlockSpec(memory_space=pl.ANY), pl.BlockSpec(memory_space=pl.ANY)),
        scratch_shapes=[pltpu.SemaphoreType.DMA((ny + 1,))],
    )(here(out), here(bub))


def solution(mesh):
    placed = (
        P(None, None, "gy", "gx"),
        P(None, None, "gy", "gx"),
        P(),
        P(None, "gx", "gy", None),
        P("gx", "gy", None),
        P("gx", "gy", None),
        P("gx", "gy", None),
        P("gx", "gy", None),
        P("gx", "gy", None),
        P("gx", "gy", None),
    )
    return jax.shard_map(
        functools.partial(shards, mesh.shape["gx"], mesh.shape["gy"]),
        mesh=mesh,
        in_specs=placed,
        out_specs=(P(None, None, "gy", "gx"), P(None, "gx", "gy", None)),
        check_vma=False,
    )
```
